32 devices in a mesh: segment: 4 (over y, x), dom: 8 (over z, core).
Axes of the slice: x: 2, y: 2, z: 4, core: 2. Of those that a mesh axis runs over, the one named last changes fastest.
Arguments:
- features: bfloat16 [4, 4096, 512], P(None, 'dom'), may hold values from -6 to 6
- send_rows: int32 [4, 8, 8, 128], P(None, 'dom'), may hold values from 0 to 511
- send_len: int32 [4, 8, 8], P(None, 'dom'), may hold values from 0 to 128, as said below
- tile_src: int32 [4, 32, 4], P(None, 'dom'), may hold values from 0 to 11
- tile_count: int32 [4, 32], P(None, 'dom'), may hold values from 1 to 4, as said below
- tile_val: bfloat16 [4, 32, 4, 128, 128], P(None, 'dom'), may hold values from -0.25 to 0.25
- w_self: bfloat16 [4, 512, 512], P('segment'), may hold values from -0.25 to 0.25
- w_neigh: bfloat16 [4, 512, 512], P('segment'), may hold values from -0.25 to 0.25
- gain: bfloat16 [4, 512], P('segment'), may hold values from 0.25 to 1.75
- bias: bfloat16 [4, 512], P('segment'), may hold values from -3 to 3
Outputs:
- acts: bfloat16 [4, 4, 4096, 512], P('segment', None, 'dom')
The draws below stay inside these ranges and needn't reach their ends.
Inputs may be any that keep to these rules, and one draw needn't show every extreme that they name: `send_len`: A partition sends nothing to itself; in every span each partition sends a full block of 128 rows to one other partition. `tile_count`: in every span one partition has 4 live tiles in each of its blocks.
All inputs are finite; a program needn't handle non-finite values.
Results may differ from the reference program's by a relative error of at most 0.0065.
Values may be sent and summed in bfloat16 or wider, within the bound.
No kernel may reach another device: no remote copies, remote signals or barrier semaphores. Data moves between devices by JAX's collectives and lax.ppermute only.
A program may use at most 64 MiB of HBM per device.

```python
import jax
import jax.numpy as jnp
from jax import lax

D = 512
TILE = 128
NB = 4
K = 4
SPANS = 4
LAYERS = 4
NODES = 4096
N_DOM = 8


def draw_send_len(key, part):
    first_key, second_key = jax.random.split(key)
    lengths = jax.random.randint(first_key, (SPANS, N_DOM, N_DOM), 0, TILE + 1)
    offset = jax.random.randint(second_key, (SPANS, N_DOM, 1), 1, N_DOM)
    sender = lax.broadcasted_iota(jnp.int32, (SPANS, N_DOM, N_DOM), 1)
    target = lax.broadcasted_iota(jnp.int32, (SPANS, N_DOM, N_DOM), 2)
    full_peer = (sender + offset) % N_DOM
    lengths = jnp.where(target == full_peer, TILE, lengths)
    return jnp.where(target == sender, 0, lengths).astype(jnp.int32)


def draw_tile_count(key, part):
    first_key, second_key, third_key = jax.random.split(key, 3)
    load_level = jax.random.randint(first_key, (SPANS, N_DOM, 1), 1, K + 1)
    drawn_raw = jax.random.randint(second_key, (SPANS, N_DOM, NB), 0, K)
    counts = 1 + drawn_raw % load_level
    busy_part = jax.random.randint(third_key, (SPANS, 1, 1), 0, N_DOM)
    partition = lax.broadcasted_iota(jnp.int32, (SPANS, N_DOM, NB), 1)
    counts = jnp.where(partition == busy_part, K, counts)
    return counts.reshape(SPANS, N_DOM * NB).astype(jnp.int32)


def with_ends(array, own_key, smallest, largest):
    dims = array.shape
    index_at = [jax.random.randint(jax.random.fold_in(own_key, axis), (), 0, dims[axis]) for axis in range(len(dims))]
    array = array.at[tuple(index_at)].set(smallest)
    longest = dims.index(max(dims))
    index_at[longest] = (index_at[longest] + 1) % dims[longest]
    return array.at[tuple(index_at)].set(largest)


def block_levels(key, dims, shards, smallest, largest):
    level = 1.0
    for dim, shards_of in shards:
        heights = jax.random.uniform(jax.random.fold_in(jax.random.fold_in(key, 6), dim), (shards_of,), jnp.float32, smallest / len(shards), largest / len(shards))
        level = level * jnp.repeat(jnp.exp(heights), dims[dim] // shards_of).reshape((-1,) + (1,) * (len(dims) - 1 - dim))
    return level


def bell_draw(rng, dims, scale, most, cuts=(), dtype=jnp.bfloat16):
    level = block_levels(rng, dims, cuts, -0.22, 0.18) if cuts else 1.0
    result = jax.random.normal(rng, dims, jnp.float32) * scale * level
    return jnp.minimum(jnp.maximum(result, -most), most).astype(dtype)


def setup_inputs(seed: int = 0) -> dict:
    arg_keys = jax.random.split(jax.random.key(seed), 11)
    features = bell_draw(arg_keys[0], (SPANS, NODES, D), 1.0, 6.0, ((1, 8),))
    send_rows = with_ends(jax.random.randint(arg_keys[1], (SPANS, N_DOM, N_DOM, TILE), 0, NB * TILE), jax.random.fold_in(arg_keys[1], 1), 0, (NB * TILE) - 1).astype(jnp.int32)
    send_len = draw_send_len(jax.random.fold_in(arg_keys[10], 71), 0)
    tile_src = with_ends(jax.random.randint(arg_keys[3], (SPANS, NODES // TILE, K), 0, NB + N_DOM), jax.random.fold_in(arg_keys[3], 1), 0, (NB + N_DOM) - 1).astype(jnp.int32)
    tile_count = draw_tile_count(jax.random.fold_in(arg_keys[10], 71), 0)
    tile_val = bell_draw(arg_keys[5], (SPANS, NODES // TILE, K, TILE, TILE), (TILE * K) ** -0.5, 0.25, ((1, 8),))
    w_self = bell_draw(arg_keys[6], (LAYERS, D, D), D ** -0.5, 0.25, ((0, 4),))
    w_neigh = bell_draw(arg_keys[7], (LAYERS, D, D), D ** -0.5, 0.25, ((0, 4),))
    gain = jnp.clip(1.0 + 0.15 * jax.random.normal(arg_keys[8], (LAYERS, D), jnp.float32), 0.25, 1.75).astype(jnp.bfloat16)
    bias = bell_draw(arg_keys[9], (LAYERS, D), 0.5, 3.0, ((0, 4),))
    return dict(features=features, send_rows=send_rows, send_len=send_len, tile_src=tile_src, tile_count=tile_count, tile_val=tile_val, w_self=w_self, w_neigh=w_neigh, gain=gain, bias=bias)


norm_eps = 1e-05

def take_rows(part_rows, part_list):
    return jnp.take(part_rows, part_list.reshape(-1), axis=0)

def part_sum(packed):
    part_sources, part_src, part_count, part_val = packed
    chosen = jnp.take(part_sources, part_src.reshape(-1), axis=0).reshape(NB, K, TILE, D).astype(jnp.float32)
    keep_tile = lax.broadcasted_iota(jnp.int32, (NB, K), 1) < part_count[:, None]
    coeffs = jnp.where(keep_tile[:, :, None, None], part_val.astype(jnp.float32), jnp.zeros((NB, K, TILE, TILE), jnp.float32))
    return jnp.einsum('bkij,bkjd->bid', coeffs, chosen)

def sage_layer(hidden, rows_c, len_c, src_c, count_c, val_c, w_one, w_two, gain_one, bias_one):
    owned = hidden.reshape(N_DOM, NB * TILE, D)
    picked = jax.vmap(take_rows)(owned, rows_c).reshape(N_DOM, N_DOM, TILE, D)
    row_live = lax.broadcasted_iota(jnp.int32, (N_DOM, N_DOM, TILE), 2) < len_c[:, :, None]
    halo = jnp.where(row_live[:, :, :, None], picked, jnp.zeros_like(picked))
    arriving = jnp.transpose(halo, (1, 0, 2, 3))
    sources = jnp.concatenate([owned.reshape(N_DOM, NB, TILE, D), arriving], axis=1)
    summed = lax.map(part_sum, (sources, src_c.reshape(N_DOM, NB, K), count_c.reshape(N_DOM, NB), val_c.reshape(N_DOM, NB, K, TILE, TILE)))
    gathered = summed.reshape(N_DOM * NB * TILE, D).astype(jnp.bfloat16)
    mixed = jnp.dot(hidden, w_one, preferred_element_type=jnp.float32) + jnp.dot(gathered, w_two, preferred_element_type=jnp.float32)
    center = mixed - lax.optimization_barrier(jnp.mean(mixed, axis=1, keepdims=True))
    spread = lax.optimization_barrier(jnp.mean(center * center, axis=1, keepdims=True))
    scaled = center * lax.rsqrt(spread + norm_eps) * gain_one.astype(jnp.float32) + bias_one.astype(jnp.float32)
    return jnp.maximum(scaled, 0.0).astype(jnp.bfloat16)

def reference(features, send_rows, send_len, tile_src, tile_count, tile_val, w_self, w_neigh, gain, bias):
    per_layer = [[] for layer_id in range(LAYERS)]
    for span_id in range(SPANS):
        hidden = features[span_id]
        for layer_id in range(LAYERS):
            hidden = sage_layer(hidden, send_rows[span_id], send_len[span_id], tile_src[span_id], tile_count[span_id], tile_val[span_id], w_self[layer_id], w_neigh[layer_id], gain[layer_id], bias[layer_id])
            per_layer[layer_id].append(hidden)
    return jnp.stack([jnp.stack(layer_acts) for layer_acts in per_layer])
```

```python
import functools

import jax
import jax.numpy as jnp
from jax import lax
from jax.experimental import pallas as pl
from jax.experimental.pallas import tpu as pltpu
from jax.sharding import PartitionSpec as P

norm_eps = 1e-05
pad_rows = 16


def select_span(array_in, span_id):
    return lax.dynamic_index_in_dim(array_in, span_id, 0, keepdims=False)


def sage_layer(inputs, span_id, graph, w_one, w_two, gain_one, bias_one):
    rows_all, lens_all, src_all, count_all, vals_all = graph
    send_list = select_span(rows_all, span_id)[0]
    send_count = select_span(lens_all, span_id)[0]
    tile_index = select_span(src_all, span_id)
    tile_total = select_span(count_all, span_id)
    tile_vals = select_span(vals_all, span_id)
    peer_count, tile_rows = send_list.shape
    feat_width = inputs.shape[1]
    block_count, tile_depth = tile_index.shape
    picked = jnp.take(inputs, send_list.reshape(-1), axis=0).reshape(
        peer_count, tile_rows, feat_width
    )
    row_live = lax.broadcasted_iota(jnp.int32, (peer_count, tile_rows), 1) < send_count[:, None]
    outgoing = jnp.where(row_live[:, :, None], picked, jnp.zeros_like(picked))
    incoming = lax.all_to_all(outgoing, "dom", split_axis=0, concat_axis=0, tiled=True)
    sources = jnp.concatenate(
        [inputs.reshape(block_count, tile_rows, feat_width), incoming], axis=0
    )
    tile_live = lax.broadcasted_iota(jnp.int32, (block_count, tile_depth), 1) < tile_total[:, None]

    def block_sum(packed):
        block_index, block_vals, block_live = packed
        chosen = jnp.take(sources, block_index, axis=0)
        masked = jnp.where(block_live[:, None, None], block_vals, jnp.zeros_like(block_vals))
        return jnp.einsum("kij,kjd->id", masked, chosen, preferred_element_type=jnp.float32)

    summed = lax.map(block_sum, (tile_index, tile_vals, tile_live))
    gathered = summed.reshape(block_count * tile_rows, feat_width).astype(jnp.bfloat16)
    mixed = jnp.dot(inputs, w_one, preferred_element_type=jnp.float32) + jnp.dot(
        gathered, w_two, preferred_element_type=jnp.float32
    )
    center = mixed - jnp.mean(mixed, axis=1, keepdims=True)
    spread = jnp.mean(center * center, axis=1, keepdims=True)
    scaled = center * lax.rsqrt(spread + norm_eps) * gain_one.astype(jnp.float32) + bias_one.astype(
        jnp.float32
    )
    return jnp.maximum(scaled, 0.0).astype(jnp.bfloat16)


def general_device(
    features, send_rows, send_len, tile_src, tile_count, tile_val, w_self, w_neigh, gain, bias
):
    segments = lax.axis_size("segment")
    segment_id = lax.axis_index("segment")
    span_total = features.shape[0]
    graph = (send_rows, send_len, tile_src, tile_count, tile_val)
    every_self, every_neigh, every_gain, every_bias = (
        lax.all_gather(w_self, "segment", axis=0, tiled=True),
        lax.all_gather(w_neigh, "segment", axis=0, tiled=True),
        lax.all_gather(gain, "segment", axis=0, tiled=True),
        lax.all_gather(bias, "segment", axis=0, tiled=True),
    )
    span_group = span_total // segments
    layers = every_self.shape[0]
    finished = []
    for item in range(span_group):
        span_id = segment_id * span_group + item
        hidden = select_span(features, span_id)
        outputs = []
        for layer_id in range(layers):
            hidden = sage_layer(
                hidden,
                span_id,
                graph,
                every_self[layer_id],
                every_neigh[layer_id],
                every_gain[layer_id],
                every_bias[layer_id],
            )
            outputs.append(hidden)
        finished.append(jnp.stack(outputs))
    dealt_out = jnp.stack(finished, axis=1)
    return lax.all_to_all(dealt_out, "segment", split_axis=0, concat_axis=1, tiled=True)


slot_xor = (0, 2, 1, 3, 6, 7, 4, 5)
slot_total = len(slot_xor)


def layer_body(dims, x_slots, t_total, first, count, out_slots, *refs):
    rows, tile, width, blocks, depth = dims
    codes, counts, place = refs[:3]
    refs = refs[3:]
    x_refs, refs = refs[: len(x_slots)], refs[len(x_slots) :]
    t_refs, refs = refs[:t_total], refs[t_total:]
    mine_w, refs = refs[:4], refs[4:]
    other_w, refs = refs[:4], refs[4:]
    list_ref, refs = refs[0], refs[1:]
    o_refs, refs = refs[: len(out_slots)], refs[len(out_slots) :]
    xs, ts, ws, src, agg, ob, sem_x, sem_t, sem_w, sem_o = refs
    hop = place[0]
    core = place[1]

    def copies_w():
        for j in range(4):
            yield j, 0, pltpu.make_async_copy(mine_w[j], ws.at[0], sem_w.at[0])
            yield j, 1, pltpu.make_async_copy(other_w[j], ws.at[1], sem_w.at[1])

    for j, _, copy in copies_w():
        @pl.when(hop == j)
        def _():
            copy.start()

    x_copies = []
    for n, (ref, slots) in enumerate(zip(x_refs, x_slots)):
        copy = pltpu.make_async_copy(
            ref, xs.at[pl.ds(slots[0] * rows, len(slots) * rows), :], sem_x.at[n]
        )
        copy.start()
        x_copies.append(copy)
    t_copies = []
    for n, ref in enumerate(t_refs):
        copy = pltpu.make_async_copy(ref, ts.at[n], sem_t.at[n])
        copy.start()
        t_copies.append(copy)
    pltpu.make_async_copy(mine_w[0], ws.at[0], sem_w.at[0]).wait()
    pltpu.make_async_copy(other_w[0], ws.at[1], sem_w.at[1]).wait()
    for copy in x_copies:
        copy.wait()
    for copy in t_copies:
        copy.wait()
    lanes = lax.broadcasted_iota(jnp.int32, (tile, rows), 1)
    gain_row = ws[0, width : width + 1, :].astype(jnp.float32)
    bias_row = ws[0, width + 1 : width + 2, :].astype(jnp.float32)

    def step(i, carry):
        slot = first + i
        x = xs[pl.ds(pl.multiple_of(slot * rows, rows), rows), :]
        src[0:rows, :] = x
        lists = list_ref[slot]
        for q in range(slot_total):
            pick = jnp.where(lanes == lists[:, q : q + 1], 1.0, 0.0).astype(jnp.bfloat16)
            block = jnp.dot(
                pick, xs[q * rows : (q + 1) * rows, :], preferred_element_type=jnp.float32
            )
            src[rows + q * tile : rows + (q + 1) * tile, :] = block.astype(jnp.bfloat16)
        for b in range(blocks):
            live = counts[slot * blocks + b]
            left = []
            right = []
            for k in range(depth):
                at = b * depth + k
                coeff = ts[i, at * tile : (at + 1) * tile, :]
                left.append(jnp.where(k < live, coeff, jnp.zeros_like(coeff)))
                code = codes[slot * blocks * depth + at]
                right.append(src[pl.ds(pl.multiple_of(code * tile, tile), tile), :])
            total = jnp.dot(
                jnp.concatenate(left, axis=1),
                jnp.concatenate(right, axis=0),
                preferred_element_type=jnp.float32,
            )
            agg[b * tile : (b + 1) * tile, :] = total.astype(jnp.bfloat16)
        pre = jnp.dot(x, ws[core, :width, :], preferred_element_type=jnp.float32) + jnp.dot(
            agg[...], ws[1 - core, :width, :], preferred_element_type=jnp.float32
        )
        center = pre - jnp.mean(pre, axis=1, keepdims=True)
        spread = jnp.mean(center * center, axis=1, keepdims=True)
        scaled = center * lax.rsqrt(spread + norm_eps) * gain_row + bias_row
        ob[i] = jnp.maximum(scaled, 0.0).astype(jnp.bfloat16)
        for n, (ref, slots) in enumerate(zip(o_refs, out_slots)):
            for m, s in enumerate(slots):
                @pl.when(slot == s)
                def _():
                    pltpu.make_async_copy(
                        ob.at[s - first], ref.at[pl.ds(m * rows, rows), :], sem_o.at[s - first]
                    ).start()
        return carry

    lax.fori_loop(0, count, step, 0)
    for n, (ref, slots) in enumerate(zip(o_refs, out_slots)):
        for m, s in enumerate(slots):
            pltpu.make_async_copy(
                ob.at[s - first], ref.at[pl.ds(m * rows, rows), :], sem_o.at[s - first]
            ).wait()


def run_layer(dims, tables, weights, hop_core, x_parts, t_parts, first, count, out_slots):
    rows, tile, width, blocks, depth = dims
    codes, counts, lists = tables
    mine, other = weights
    x_slots = tuple(slots for _, slots in x_parts)
    anyspace = pl.BlockSpec(memory_space=pl.ANY)
    smem = pl.BlockSpec(memory_space=pltpu.SMEM)
    vmem = pl.BlockSpec(memory_space=pltpu.VMEM)
    bf16 = jnp.bfloat16
    n_any = len(x_parts) + len(t_parts) + 8
    body = functools.partial(layer_body, dims, x_slots, len(t_parts), first, count, out_slots)
    return pl.pallas_call(
        body,
        out_shape=[
            jax.ShapeDtypeStruct((len(slots) * rows, width), bf16) for slots in out_slots
        ],
        in_specs=[smem] * 3 + [anyspace] * n_any + [vmem],
        out_specs=[anyspace] * len(out_slots),
        scratch_shapes=[
            pltpu.VMEM((slot_total * rows, width), bf16),
            pltpu.VMEM((count, blocks * depth * tile, tile), bf16),
            pltpu.VMEM((2, width + pad_rows, width), bf16),
            pltpu.VMEM((rows + slot_total * tile, width), bf16),
            pltpu.VMEM((rows, width), bf16),
            pltpu.VMEM((count, rows, width), bf16),
            pltpu.SemaphoreType.DMA((len(x_parts),)),
            pltpu.SemaphoreType.DMA((count,)),
            pltpu.SemaphoreType.DMA((2,)),
            pltpu.SemaphoreType.DMA((count,)),
        ],
        name="layer_rows",
    )(
        codes, counts, hop_core, *[a for a, _ in x_parts], *t_parts, *mine, *other, lists
    )


def join_body(segments, rows, refs_in, where_at, own, recv_mid, recv_edge, out, sem):
    raise NotImplementedError


def assemble(dims, segments, place, own, mids, edges):
    rows, tile, width, blocks, depth = dims
    anyspace = pl.BlockSpec(memory_space=pl.ANY)
    smem = pl.BlockSpec(memory_space=pltpu.SMEM)
    flat = []
    for l in range(segments):
        flat += list(own[l]) + list(mids[l]) + list(edges[l])

    def body(place_ref, *refs):
        out, sem = refs[-2:]
        ins = refs[:-2]
        column = place_ref[0]
        edge = place_ref[1]
        per = 2 + 2 * (segments - 1)
        for l in range(segments):
            group = ins[l * per : (l + 1) * per]
            for e in range(2):
                @pl.when((column == l) & (edge == e))
                def _():
                    for step in range(segments):
                        if step == 0:
                            ref = group[e]
                        else:
                            ref = group[2 + e * (segments - 1) + step - 1]
                        pltpu.make_async_copy(ref, out.at[l ^ step], sem.at[l ^ step]).start()
        for c in range(segments):
            pltpu.make_async_copy(ins[0], out.at[c], sem.at[c]).wait()

    return pl.pallas_call(
        body,
        out_shape=jax.ShapeDtypeStruct((segments, rows, width), jnp.bfloat16),
        in_specs=[smem] + [anyspace] * len(flat),
        out_specs=anyspace,
        scratch_shapes=[pltpu.SemaphoreType.DMA((segments,))],
        name="join_layers",
    )(place, *flat)


def line_device(
    features, send_rows, send_len, tile_src, tile_count, tile_val, w_self, w_neigh, gain, bias
):
    segments = lax.axis_size("segment")
    parts = lax.axis_size("dom")
    column = lax.axis_index("segment")
    part = lax.axis_index("dom")
    core = part % 2
    rows, width = features.shape[1:]
    blocks, depth, tile = tile_val.shape[1:4]
    dims = (rows, tile, width, blocks, depth)
    layers = segments
    mid = [p for p in range(parts) if 0 < p // 2 < parts // 2 - 1]
    rim = [p for p in range(parts) if p not in mid]
    axes = ("segment", "dom")

    def along(array, which, change):
        pairs = [
            (k * parts + p, k * parts + (p ^ change)) for k in range(segments) for p in which
        ]
        return lax.ppermute(array, axes, pairs)

    def gather_slots(own):
        rim_in = along(own, rim, 2)
        far_mid = along(own, mid, 6)
        far_rim = along(rim_in, mid, 6)
        swap = lambda a: along(a, mid, 1)
        return [own, rim_in, swap(own), swap(rim_in), far_mid, swap(far_mid), far_rim, swap(far_rim)]

    lists = select_span(send_rows, column)[0]
    lens = select_span(send_len, column)[0]
    srcs = select_span(tile_src, column)
    cnts = select_span(tile_count, column)
    live_row = lax.broadcasted_iota(jnp.int32, lists.shape, 1) < lens[:, None]
    lists = jnp.where(live_row, lists, -1)
    live_tile = lax.broadcasted_iota(jnp.int32, srcs.shape, 1) < cnts[:, None]
    srcs = jnp.where(live_tile, srcs, 0)
    packed = jnp.concatenate([srcs.reshape(-1), cnts])
    packed = jnp.pad(packed, (0, tile - packed.shape[0]))[None]
    packed = jnp.concatenate([lists, packed, jnp.zeros((7, tile), jnp.int32)], axis=0)
    tabs = jnp.stack(gather_slots(packed))
    offs = jnp.array(slot_xor, jnp.int32)
    back = [0] * slot_total
    for n, o in enumerate(slot_xor):
        back[o] = n
    back = jnp.array(back, jnp.int32)
    list_cols = jnp.take(tabs[:, :parts, :], part ^ offs, axis=1)
    list_cols = jnp.transpose(list_cols, (1, 2, 0))
    codes = tabs[:, parts, : blocks * depth]
    codes = jnp.where(
        codes < blocks,
        codes,
        blocks + jnp.take(back, jnp.bitwise_xor(jnp.maximum(codes - blocks, 0), part)),
    )
    counts = tabs[:, parts, blocks * depth : blocks * depth + blocks]
    tables = (codes.reshape(-1), counts.reshape(-1), list_cols)

    chosen = jnp.where(core == 0, w_self[0], w_neigh[0])
    filler = jnp.zeros((pad_rows - 2, width), jnp.bfloat16)
    payload = jnp.concatenate([chosen, gain, bias, filler], axis=0)

    def across(array, which, change, target=None):
        pairs = [
            (k * parts + p, (k ^ change) * parts + p)
            for k in range(segments)
            for p in which
            if target is None or k ^ change == target
        ]
        return lax.ppermute(array, axes, pairs)

    mine = [payload] + [across(payload, mid, h) for h in range(1, segments)]
    other = [along(a, mid, 1) for a in mine]
    weights = (mine, other)

    feats = gather_slots(select_span(features, column))
    vals = gather_slots(select_span(tile_val, column).reshape(blocks * depth * tile, tile))

    own, mids, edges = [], [], []
    x_parts = [(a, (n,)) for n, a in enumerate(feats)]
    last = layers - 1
    for l in range(layers):
        hop_core = jnp.stack([jnp.bitwise_xor(column, l), core]).astype(jnp.int32)
        call = functools.partial(run_layer, dims, tables, weights, hop_core)
        if l == 0:
            near, rim_out, rest = call(
                x_parts, vals[:6], 0, 6, ((0,), (1,), (2, 3, 4, 5))
            )
            (tail,) = call(x_parts, vals[6:], 6, 2, ((6, 7),))
            x_parts = [(near, (0,)), (rim_out, (1,)), (rest, (2, 3, 4, 5)), (tail, (6, 7))]
        elif l < last:
            near, rim_out, rest = call(
                x_parts, vals, 0, 8, ((0,), (1,), (2, 3, 4, 5, 6, 7))
            )
            x_parts = [(near, (0,)), (rim_out, (1,)), (rest, (2, 3, 4, 5, 6, 7))]
        else:
            near, rim_out = call(x_parts, vals[:2], 0, 2, ((0,), (1,)))
        moved = along(rim_out, mid, 2)
        own.append((near, moved))
        mids.append([across(near, mid, h, l) for h in range(1, segments)])
        edges.append([across(moved, rim, h, l) for h in range(1, segments)])

    is_rim = jnp.logical_or(part // 2 == 0, part // 2 == parts // 2 - 1)
    place = jnp.stack([column, is_rim.astype(jnp.int32)]).astype(jnp.int32)
    return assemble(dims, segments, place, own, mids, edges)[None]


def solution(mesh):
    in_specs = (
        P(None, "dom", None),
        P(None, "dom", None, None),
        P(None, "dom", None),
        P(None, "dom", None),
        P(None, "dom"),
        P(None, "dom", None, None, None),
        P("segment", None, None),
        P("segment", None, None),
        P("segment", None),
        P("segment", None),
    )
    out_specs = P("segment", None, "dom", None)
    short_line = mesh.shape["dom"] == slot_total and mesh.shape["segment"] == 4
    device = line_device if short_line else general_device
    return jax.shard_map(
        device, mesh=mesh, in_specs=in_specs, out_specs=out_specs, check_vma=False
    )
```

```python
import functools

import jax
import jax.numpy as jnp
from jax import lax
from jax.experimental import pallas as pl
from jax.experimental.pallas import tpu as pltpu
from jax.sharding import PartitionSpec as P

norm_eps = 1e-05
pad_rows = 16


def select_span(array_in, span_id):
    return lax.dynamic_index_in_dim(array_in, span_id, 0, keepdims=False)


def sage_layer(inputs, span_id, graph, w_one, w_two, gain_one, bias_one):
    rows_all, lens_all, src_all, count_all, vals_all = graph
    send_list = select_span(rows_all, span_id)[0]
    send_count = select_span(lens_all, span_id)[0]
    tile_index = select_span(src_all, span_id)
    tile_total = select_span(count_all, span_id)
    tile_vals = select_span(vals_all, span_id)
    peer_count, tile_rows = send_list.shape
    feat_width = inputs.shape[1]
    block_count, tile_depth = tile_index.shape
    picked = jnp.take(inputs, send_list.reshape(-1), axis=0).reshape(
        peer_count, tile_rows, feat_width
    )
    row_live = lax.broadcasted_iota(jnp.int32, (peer_count, tile_rows), 1) < send_count[:, None]
    outgoing = jnp.where(row_live[:, :, None], picked, jnp.zeros_like(picked))
    incoming = lax.all_to_all(outgoing, "dom", split_axis=0, concat_axis=0, tiled=True)
    sources = jnp.concatenate(
        [inputs.reshape(block_count, tile_rows, feat_width), incoming], axis=0
    )
    tile_live = lax.broadcasted_iota(jnp.int32, (block_count, tile_depth), 1) < tile_total[:, None]

    def block_sum(packed):
        block_index, block_vals, block_live = packed
        chosen = jnp.take(sources, block_index, axis=0)
        masked = jnp.where(block_live[:, None, None], block_vals, jnp.zeros_like(block_vals))
        return jnp.einsum("kij,kjd->id", masked, chosen, preferred_element_type=jnp.float32)

    summed = lax.map(block_sum, (tile_index, tile_vals, tile_live))
    gathered = summed.reshape(block_count * tile_rows, feat_width).astype(jnp.bfloat16)
    mixed = jnp.dot(inputs, w_one, preferred_element_type=jnp.float32) + jnp.dot(
        gathered, w_two, preferred_element_type=jnp.float32
    )
    center = mixed - jnp.mean(mixed, axis=1, keepdims=True)
    spread = jnp.mean(center * center, axis=1, keepdims=True)
    scaled = center * lax.rsqrt(spread + norm_eps) * gain_one.astype(jnp.float32) + bias_one.astype(
        jnp.float32
    )
    return jnp.maximum(scaled, 0.0).astype(jnp.bfloat16)


def general_device(
    features, send_rows, send_len, tile_src, tile_count, tile_val, w_self, w_neigh, gain, bias
):
    segments = lax.axis_size("segment")
    segment_id = lax.axis_index("segment")
    span_total = features.shape[0]
    graph = (send_rows, send_len, tile_src, tile_count, tile_val)
    every_self, every_neigh, every_gain, every_bias = (
        lax.all_gather(w_self, "segment", axis=0, tiled=True),
        lax.all_gather(w_neigh, "segment", axis=0, tiled=True),
        lax.all_gather(gain, "segment", axis=0, tiled=True),
        lax.all_gather(bias, "segment", axis=0, tiled=True),
    )
    span_group = span_total // segments
    layers = every_self.shape[0]
    finished = []
    for item in range(span_group):
        span_id = segment_id * span_group + item
        hidden = select_span(features, span_id)
        outputs = []
        for layer_id in range(layers):
            hidden = sage_layer(
                hidden,
                span_id,
                graph,
                every_self[layer_id],
                every_neigh[layer_id],
                every_gain[layer_id],
                every_bias[layer_id],
            )
            outputs.append(hidden)
        finished.append(jnp.stack(outputs))
    dealt_out = jnp.stack(finished, axis=1)
    return lax.all_to_all(dealt_out, "segment", split_axis=0, concat_axis=1, tiled=True)


slot_xor = (0, 2, 6, 4, 1, 3, 7, 5)
slot_total = len(slot_xor)
half = slot_total // 2


def layer_body(dims, x_slots, t_total, first, out_slots, *refs):
    rows, tile, width, blocks, depth = dims
    count = t_total
    codes, place = refs[:2]
    refs = refs[2:]
    x_refs, refs = refs[: len(x_slots)], refs[len(x_slots) :]
    t_refs, refs = refs[:t_total], refs[t_total:]
    mine_w, other_w, list_ref = refs[:3]
    refs = refs[3:]
    o_refs, refs = refs[: len(out_slots)], refs[len(out_slots) :]
    xs, ts, ws, src, agg, ob, sem_x, sem_t, sem_w, sem_o = refs
    hop = place[0]
    core = place[1]

    w_copies = [
        pltpu.make_async_copy(ref.at[hop], ws.at[n], sem_w.at[n])
        for n, ref in enumerate((mine_w, other_w))
    ]
    x_copies = []
    for n, (ref, slots) in enumerate(zip(x_refs, x_slots)):
        size = len(slots) * rows
        x_copies.append(
            pltpu.make_async_copy(
                ref.at[pl.ds(0, size), :], xs.at[pl.ds(slots[0] * rows, size), :], sem_x.at[n]
            )
        )
    t_copies = [
        pltpu.make_async_copy(ref, ts.at[n], sem_t.at[n]) for n, ref in enumerate(t_refs)
    ]
    for copy in x_copies + t_copies + w_copies:
        copy.start()
    for copy in x_copies + w_copies:
        copy.wait()
    lanes = lax.broadcasted_iota(jnp.int32, (tile, rows), 1)
    gain_row = ws[0, width : width + 1, :].astype(jnp.float32)
    bias_row = ws[0, width + 1 : width + 2, :].astype(jnp.float32)

    def step(i, carry):
        slot = first + i
        x = xs[pl.ds(pl.multiple_of(slot * rows, rows), rows), :]
        src[0:rows, :] = x
        lists = list_ref[slot]
        for q in range(slot_total):
            pick = jnp.where(lanes == lists[:, q : q + 1], 1.0, 0.0).astype(jnp.bfloat16)
            block = jnp.dot(
                pick, xs[q * rows : (q + 1) * rows, :], preferred_element_type=jnp.float32
            )
            src[rows + q * tile : rows + (q + 1) * tile, :] = block.astype(jnp.bfloat16)
        pltpu.make_async_copy(t_refs[0], ts.at[i], sem_t.at[i]).wait()
        for b in range(blocks):
            right = []
            for k in range(depth):
                code = codes[(slot * blocks + b) * depth + k]
                right.append(src[pl.ds(pl.multiple_of(code * tile, tile), tile), :])
            total = jnp.dot(
                ts[i, b * tile : (b + 1) * tile, :],
                jnp.concatenate(right, axis=0),
                preferred_element_type=jnp.float32,
            )
            agg[b * tile : (b + 1) * tile, :] = total.astype(jnp.bfloat16)
        pre = jnp.dot(x, ws[core, :width, :], preferred_element_type=jnp.float32) + jnp.dot(
            agg[...], ws[1 - core, :width, :], preferred_element_type=jnp.float32
        )
        center = pre - jnp.mean(pre, axis=1, keepdims=True)
        spread = jnp.mean(center * center, axis=1, keepdims=True)
        scaled = center * lax.rsqrt(spread + norm_eps) * gain_row + bias_row
        ob[i] = jnp.maximum(scaled, 0.0).astype(jnp.bfloat16)
        for n, (ref, slots) in enumerate(zip(o_refs, out_slots)):
            for m, s in enumerate(slots):
                @pl.when(slot == s)
                def _():
                    pltpu.make_async_copy(
                        ob.at[s - first], ref.at[pl.ds(m * rows, rows), :], sem_o.at[n, m]
                    ).start()
        return carry

    lax.fori_loop(0, count, step, 0)
    for n, (ref, slots) in enumerate(zip(o_refs, out_slots)):
        for m, s in enumerate(slots):
            pltpu.make_async_copy(
                ob.at[s - first], ref.at[pl.ds(m * rows, rows), :], sem_o.at[n, m]
            ).wait()


def run_layer(dims, tables, weights, hop_core, x_parts, t_parts, first, out_slots):
    rows, tile, width, blocks, depth = dims
    codes, lists = tables
    count = len(t_parts)
    x_slots = tuple(slots for _, slots in x_parts)
    anyspace = pl.BlockSpec(memory_space=pl.ANY)
    smem = pl.BlockSpec(memory_space=pltpu.SMEM)
    vmem = pl.BlockSpec(memory_space=pltpu.VMEM)
    bf16 = jnp.bfloat16
    n_any = len(x_parts) + len(t_parts) + 2
    body = functools.partial(layer_body, dims, x_slots, count, first, out_slots)
    most = max(len(slots) for slots in out_slots)
    macs = count * rows * width * (2 * width + depth * tile) + count * slot_total * tile * rows * width
    return pl.pallas_call(
        body,
        out_shape=[
            jax.ShapeDtypeStruct((len(slots) * rows, width), bf16) for slots in out_slots
        ],
        in_specs=[smem] * 2 + [anyspace] * n_any + [vmem],
        out_specs=[anyspace] * len(out_slots),
        scratch_shapes=[
            pltpu.VMEM((slot_total * rows, width), bf16),
            pltpu.VMEM((count, rows, depth * tile), bf16),
            pltpu.VMEM((2, width + pad_rows, width), bf16),
            pltpu.VMEM((rows + slot_total * tile, width), bf16),
            pltpu.VMEM((rows, width), bf16),
            pltpu.VMEM((count, rows, width), bf16),
            pltpu.SemaphoreType.DMA((len(x_parts),)),
            pltpu.SemaphoreType.DMA((count,)),
            pltpu.SemaphoreType.DMA((2,)),
            pltpu.SemaphoreType.DMA((len(out_slots), most)),
        ],
        cost_estimate=pl.CostEstimate(
            flops=2 * macs,
            transcendentals=count * rows,
            bytes_accessed=2 * rows * width * (slot_total + 2 * count + 2),
        ),
        name="layer_rows",
    )(codes, hop_core, *[a for a, _ in x_parts], *t_parts, *weights, lists)


def join_layers(dims, segments, place, groups):
    rows, tile, width, blocks, depth = dims
    anyspace = pl.BlockSpec(memory_space=pl.ANY)
    smem = pl.BlockSpec(memory_space=pltpu.SMEM)
    flat = []
    index = {}
    for l, group in enumerate(groups):
        for e, arrays in enumerate(group):
            for h, array in enumerate(arrays):
                spot = [n for n, a in enumerate(flat) if a is array]
                index[l, e, h] = spot[0] if spot else len(flat)
                if not spot:
                    flat.append(array)

    def body(place_ref, *refs):
        out, hold, sem_in, sem_out = refs[-4:]
        ins = refs[:-4]
        for l, group in enumerate(groups):
            for e in range(len(group)):
                here = place_ref[0] == l
                if len(group) > 1:
                    here = here & (place_ref[1] == e)

                @pl.when(here)
                def _():
                    for h in range(segments):
                        pltpu.make_async_copy(
                            ins[index[l, e, h]], hold.at[l ^ h], sem_in.at[l ^ h]
                        ).start()
        for c in range(segments):
            pltpu.make_async_copy(ins[0], hold.at[c], sem_in.at[c]).wait()
            pltpu.make_async_copy(hold.at[c], out.at[c], sem_out.at[c]).start()
        for c in range(segments):
            pltpu.make_async_copy(hold.at[c], out.at[c], sem_out.at[c]).wait()

    return pl.pallas_call(
        body,
        out_shape=jax.ShapeDtypeStruct((segments, rows, width), jnp.bfloat16),
        in_specs=[smem] + [anyspace] * len(flat),
        out_specs=anyspace,
        scratch_shapes=[
            pltpu.VMEM((segments, rows, width), jnp.bfloat16),
            pltpu.SemaphoreType.DMA((segments,)),
            pltpu.SemaphoreType.DMA((segments,)),
        ],
        name="join_layers",
    )(place, *flat)


def line_device(
    features, send_rows, send_len, tile_src, tile_count, tile_val, w_self, w_neigh, gain, bias
):
    segments = lax.axis_size("segment")
    parts = lax.axis_size("dom")
    column = lax.axis_index("segment")
    part = lax.axis_index("dom")
    core = part % 2
    rows, width = features.shape[1:]
    blocks, depth, tile = tile_val.shape[1:4]
    dims = (rows, tile, width, blocks, depth)
    layers = segments
    bf16 = jnp.bfloat16
    mid = [p for p in range(parts) if 0 < p // 2 < parts // 2 - 1]
    rim = [p for p in range(parts) if p not in mid]
    axes = ("segment", "dom")

    def along(array, which, change):
        pairs = [
            (k * parts + p, k * parts + (p ^ change)) for k in range(segments) for p in which
        ]
        return lax.ppermute(array, axes, pairs)

    def across(array, which, change, target=None):
        pairs = [
            (k * parts + p, (k ^ change) * parts + p)
            for k in range(segments)
            for p in which
            if target is None or k ^ change == target
        ]
        return lax.ppermute(array, axes, pairs)

    lists = select_span(send_rows, column)[0]
    lens = select_span(send_len, column)[0]
    srcs = select_span(tile_src, column)
    cnts = select_span(tile_count, column)
    live_row = lax.broadcasted_iota(jnp.int32, lists.shape, 1) < lens[:, None]
    lists = jnp.where(live_row, lists + 1, 0).reshape(-1, width)
    live_tile = lax.broadcasted_iota(jnp.int32, srcs.shape, 1) < cnts[:, None]
    codes = jnp.where(live_tile, srcs, 0).reshape(-1)
    codes = jnp.pad(codes, (0, width - codes.shape[0]))[None]
    list_rows = lists.shape[0]
    notes = jnp.concatenate([lists // 16, lists % 16, codes], axis=0)
    notes = jnp.pad(notes, ((0, pad_rows - notes.shape[0]), (0, 0))).astype(bf16)
    feat_own = jnp.concatenate([select_span(features, column), notes], axis=0)
    feat_rim = along(feat_own, rim, 2)
    feat_far = along(feat_own, mid, 6)
    feat_far_rim = along(feat_rim, mid, 6)
    feats = [feat_own, feat_rim, feat_far, feat_far_rim]
    feats = feats + [along(a, mid, 1) for a in feats]

    val_own = select_span(tile_val, column)
    val_own = jnp.where(live_tile[:, :, None, None], val_own, jnp.zeros_like(val_own))
    val_own = jnp.transpose(val_own, (0, 2, 1, 3)).reshape(blocks * tile, depth * tile)
    val_rim = along(val_own, rim, 2)
    val_far = along(val_own, mid, 6)
    val_far_rim = along(val_rim, mid, 6)
    vals = [val_own, val_rim, val_far, val_far_rim]

    tabs = jnp.stack([a[rows : rows + 2 * list_rows + 1] for a in feats]).astype(jnp.int32)
    offs = jnp.array(slot_xor, jnp.int32)
    back = [0] * slot_total
    for n, o in enumerate(slot_xor):
        back[o] = n
    back = jnp.array(back, jnp.int32)
    lists = tabs[:, :list_rows] * 16 + tabs[:, list_rows : 2 * list_rows] - 1
    lists = lists.reshape(slot_total, parts, tile)
    list_cols = jnp.transpose(jnp.take(lists, part ^ offs, axis=1), (1, 2, 0))
    codes = tabs[:, 2 * list_rows, : blocks * depth]
    codes = jnp.where(
        codes < blocks,
        codes,
        blocks + jnp.take(back, jnp.bitwise_xor(jnp.maximum(codes - blocks, 0), part)),
    )
    tables = (codes.reshape(-1), list_cols)

    chosen = jnp.where(core == 0, w_self[0], w_neigh[0])
    filler = jnp.zeros((pad_rows - 2, width), bf16)
    payload = jnp.concatenate([chosen, gain, bias, filler], axis=0)
    mine = jnp.stack([payload] + [across(payload, mid, h) for h in range(1, segments)])
    weights = (mine, along(mine, mid, 1))

    is_rim = jnp.logical_or(part // 2 == 0, part // 2 == parts // 2 - 1)
    groups = []
    x_parts = [(a, (n,)) for n, a in enumerate(feats)]
    last = layers - 1
    for l in range(layers):
        hop_core = jnp.stack([jnp.bitwise_xor(column, l), core]).astype(jnp.int32)
        call = functools.partial(run_layer, dims, tables, weights, hop_core)
        if l == 0:
            near, rim_out, full = call(x_parts, vals[:3], 0, ((0,), (1,), (0, 1, 2)))
            (extra,) = call(x_parts, vals[3:], 3, ((3,),))
            x_parts = [
                (full, (0, 1, 2)),
                (extra, (3,)),
                (along(full, mid, 1), (4, 5, 6)),
                (along(extra, mid, 1), (7,)),
            ]
        elif l < last:
            near, rim_out, full = call(x_parts, vals, 0, ((0,), (1,), (0, 1, 2, 3)))
            x_parts = [(full, (0, 1, 2, 3)), (along(full, mid, 1), (4, 5, 6, 7))]
        else:
            near, rim_out = call(x_parts, vals[:2], 0, ((0,), (1,)))
        moved = along(rim_out, mid, 2)
        if l < last:
            ready = jnp.where(is_rim, moved, near)
            groups.append(
                ([ready] + [across(ready, range(parts), h, l) for h in range(1, segments)],)
            )
        else:
            groups.append(
                (
                    [near] + [across(near, mid, h, l) for h in range(1, segments)],
                    [moved] + [across(moved, rim, h, l) for h in range(1, segments)],
                )
            )

    place = jnp.stack([column, is_rim.astype(jnp.int32)]).astype(jnp.int32)
    return join_layers(dims, segments, place, groups)[None]


def solution(mesh):
    in_specs = (
        P(None, "dom", None),
        P(None, "dom", None, None),
        P(None, "dom", None),
        P(None, "dom", None),
        P(None, "dom"),
        P(None, "dom", None, None, None),
        P("segment", None, None),
        P("segment", None, None),
        P("segment", None),
        P("segment", None),
    )
    out_specs = P("segment", None, "dom", None)
    short_line = mesh.shape["dom"] == slot_total and mesh.shape["segment"] == 4
    device = line_device if short_line else general_device
    return jax.shard_map(
        device, mesh=mesh, in_specs=in_specs, out_specs=out_specs, check_vma=False
    )
```

```python
import functools

import jax
import jax.numpy as jnp
from jax import lax
from jax.experimental import pallas as pl
from jax.experimental.pallas import tpu as pltpu
from jax.sharding import PartitionSpec as P


norm_eps = 1e-05
pad_rows = 16


def select_span(array_in, span_id):
    return lax.dynamic_index_in_dim(array_in, span_id, 0, keepdims=False)


def sage_layer(inputs, span_id, graph, w_one, w_two, gain_one, bias_one):
    rows_all, lens_all, src_all, count_all, vals_all = graph
    send_list = select_span(rows_all, span_id)[0]
    send_count = select_span(lens_all, span_id)[0]
    tile_index = select_span(src_all, span_id)
    tile_total = select_span(count_all, span_id)
    tile_vals = select_span(vals_all, span_id)
    peer_count, tile_rows = send_list.shape
    feat_width = inputs.shape[1]
    block_count, tile_depth = tile_index.shape
    picked = jnp.take(inputs, send_list.reshape(-1), axis=0).reshape(
        peer_count, tile_rows, feat_width
    )
    row_live = lax.broadcasted_iota(jnp.int32, (peer_count, tile_rows), 1) < send_count[:, None]
    outgoing = jnp.where(row_live[:, :, None], picked, jnp.zeros_like(picked))
    incoming = lax.all_to_all(outgoing, "dom", split_axis=0, concat_axis=0, tiled=True)
    sources = jnp.concatenate(
        [inputs.reshape(block_count, tile_rows, feat_width), incoming], axis=0
    )
    tile_live = lax.broadcasted_iota(jnp.int32, (block_count, tile_depth), 1) < tile_total[:, None]

    def block_sum(packed):
        block_index, block_vals, block_live = packed
        chosen = jnp.take(sources, block_index, axis=0)
        masked = jnp.where(block_live[:, None, None], block_vals, jnp.zeros_like(block_vals))
        return jnp.einsum("kij,kjd->id", masked, chosen, preferred_element_type=jnp.float32)

    summed = lax.map(block_sum, (tile_index, tile_vals, tile_live))
    gathered = summed.reshape(block_count * tile_rows, feat_width).astype(jnp.bfloat16)
    mixed = jnp.dot(inputs, w_one, preferred_element_type=jnp.float32) + jnp.dot(
        gathered, w_two, preferred_element_type=jnp.float32
    )
    center = mixed - jnp.mean(mixed, axis=1, keepdims=True)
    spread = jnp.mean(center * center, axis=1, keepdims=True)
    scaled = center * lax.rsqrt(spread + norm_eps) * gain_one.astype(jnp.float32) + bias_one.astype(
        jnp.float32
    )
    return jnp.maximum(scaled, 0.0).astype(jnp.bfloat16)


def general_device(
    features, send_rows, send_len, tile_src, tile_count, tile_val, w_self, w_neigh, gain, bias
):
    segments = lax.axis_size("segment")
    segment_id = lax.axis_index("segment")
    span_total = features.shape[0]
    graph = (send_rows, send_len, tile_src, tile_count, tile_val)
    every_self, every_neigh, every_gain, every_bias = (
        lax.all_gather(w_self, "segment", axis=0, tiled=True),
        lax.all_gather(w_neigh, "segment", axis=0, tiled=True),
        lax.all_gather(gain, "segment", axis=0, tiled=True),
        lax.all_gather(bias, "segment", axis=0, tiled=True),
    )
    span_group = span_total // segments
    layers = every_self.shape[0]
    finished = []
    for item in range(span_group):
        span_id = segment_id * span_group + item
        hidden = select_span(features, span_id)
        outputs = []
        for layer_id in range(layers):
            hidden = sage_layer(
                hidden,
                span_id,
                graph,
                every_self[layer_id],
                every_neigh[layer_id],
                every_gain[layer_id],
                every_bias[layer_id],
            )
            outputs.append(hidden)
        finished.append(jnp.stack(outputs))
    dealt_out = jnp.stack(finished, axis=1)
    return lax.all_to_all(dealt_out, "segment", split_axis=0, concat_axis=1, tiled=True)


slot_xor = (0, 2, 6, 4, 1, 3, 7, 5)
slot_total = len(slot_xor)


def layer_body(dims, x_spots, t_spots, total_refs, first, out_slots, *refs):
    rows, tile, width, blocks, depth = dims
    count = len(t_spots)
    codes, place = refs[:2]
    refs = refs[2:]
    data, refs = refs[:total_refs], refs[total_refs:]
    mine_w, other_w, list_ref = refs[:3]
    refs = refs[3:]
    o_refs, refs = refs[: len(out_slots)], refs[len(out_slots) :]
    xs, ts, ws, src, agg, ob, sem_x, sem_t, sem_w, sem_o = refs
    hop = place[0]
    core = place[1]

    w_copies = [
        pltpu.make_async_copy(ref.at[hop], ws.at[n], sem_w.at[n])
        for n, ref in enumerate((mine_w, other_w))
    ]
    x_copies = []
    for n, (at, base, slots) in enumerate(x_spots):
        size = len(slots) * rows
        x_copies.append(
            pltpu.make_async_copy(
                data[at].at[pl.ds(base, size), :],
                xs.at[pl.ds(slots[0] * rows, size), :],
                sem_x.at[n],
            )
        )
    t_copies = [
        pltpu.make_async_copy(data[at].at[pl.ds(base, rows), :], ts.at[n], sem_t.at[n])
        for n, (at, base) in enumerate(t_spots)
    ]
    for copy in x_copies + t_copies + w_copies:
        copy.start()
    for copy in x_copies + w_copies:
        copy.wait()
    lanes = lax.broadcasted_iota(jnp.int32, (tile, rows), 1)
    gain_row = ws[0, width : width + 1, :].astype(jnp.float32)
    bias_row = ws[0, width + 1 : width + 2, :].astype(jnp.float32)

    def step(i, carry):
        slot = first + i
        x = xs[pl.ds(pl.multiple_of(slot * rows, rows), rows), :]
        src[0:rows, :] = x
        lists = list_ref[slot]
        for q in range(slot_total):
            pick = jnp.where(lanes == lists[:, q : q + 1], 1.0, 0.0).astype(jnp.bfloat16)
            block = jnp.dot(
                pick, xs[q * rows : (q + 1) * rows, :], preferred_element_type=jnp.float32
            )
            src[rows + q * tile : rows + (q + 1) * tile, :] = block.astype(jnp.bfloat16)
        pltpu.make_async_copy(data[0].at[pl.ds(0, rows), :], ts.at[i], sem_t.at[i]).wait()
        for b in range(blocks):
            right = []
            for k in range(depth):
                code = codes[(slot * blocks + b) * depth + k]
                right.append(src[pl.ds(pl.multiple_of(code * tile, tile), tile), :])
            total = jnp.dot(
                ts[i, b * tile : (b + 1) * tile, :],
                jnp.concatenate(right, axis=0),
                preferred_element_type=jnp.float32,
            )
            agg[b * tile : (b + 1) * tile, :] = total.astype(jnp.bfloat16)
        pre = jnp.dot(x, ws[core, :width, :], preferred_element_type=jnp.float32) + jnp.dot(
            agg[...], ws[1 - core, :width, :], preferred_element_type=jnp.float32
        )
        center = pre - jnp.mean(pre, axis=1, keepdims=True)
        spread = jnp.mean(center * center, axis=1, keepdims=True)
        scaled = center * lax.rsqrt(spread + norm_eps) * gain_row + bias_row
        ob[i] = jnp.maximum(scaled, 0.0).astype(jnp.bfloat16)
        for n, (ref, slots) in enumerate(zip(o_refs, out_slots)):
            for m, s in enumerate(slots):
                @pl.when(slot == s)
                def _():
                    pltpu.make_async_copy(
                        ob.at[s - first], ref.at[pl.ds(m * rows, rows), :], sem_o.at[n, m]
                    ).start()
        return carry

    lax.fori_loop(0, count, step, 0)
    for n, (ref, slots) in enumerate(zip(o_refs, out_slots)):
        for m, s in enumerate(slots):
            pltpu.make_async_copy(
                ob.at[s - first], ref.at[pl.ds(m * rows, rows), :], sem_o.at[n, m]
            ).wait()


def run_layer(dims, tables, weights, hop_core, x_parts, t_parts, first, out_slots):
    rows, tile, width, _, depth = dims
    codes, lists = tables
    count = len(t_parts)
    flat = []

    def spot(array):
        for n, have in enumerate(flat):
            if have is array:
                return n
        flat.append(array)
        return len(flat) - 1

    x_spots = tuple((spot(a), base, slots) for a, base, slots in x_parts)
    t_spots = tuple((spot(a), base) for a, base in t_parts)
    anyspace = pl.BlockSpec(memory_space=pl.ANY)
    smem = pl.BlockSpec(memory_space=pltpu.SMEM)
    vmem = pl.BlockSpec(memory_space=pltpu.VMEM)
    bf16 = jnp.bfloat16
    n_any = len(flat) + 2
    body = functools.partial(layer_body, dims, x_spots, t_spots, len(flat), first, out_slots)
    most = max(len(slots) for slots in out_slots)
    macs = count * rows * width * (2 * width + depth * tile) + count * slot_total * tile * rows * width
    return pl.pallas_call(
        body,
        out_shape=[
            jax.ShapeDtypeStruct((len(slots) * rows, width), bf16) for slots in out_slots
        ],
        in_specs=[smem] * 2 + [anyspace] * n_any + [vmem],
        out_specs=[anyspace] * len(out_slots),
        scratch_shapes=[
            pltpu.VMEM((slot_total * rows, width), bf16),
            pltpu.VMEM((count, rows, depth * tile), bf16),
            pltpu.VMEM((2, width + pad_rows, width), bf16),
            pltpu.VMEM((rows + slot_total * tile, width), bf16),
            pltpu.VMEM((rows, width), bf16),
            pltpu.VMEM((count, rows, width), bf16),
            pltpu.SemaphoreType.DMA((len(x_parts),)),
            pltpu.SemaphoreType.DMA((count,)),
            pltpu.SemaphoreType.DMA((2,)),
            pltpu.SemaphoreType.DMA((len(out_slots), most)),
        ],
        cost_estimate=pl.CostEstimate(
            flops=2 * macs,
            transcendentals=count * rows,
            bytes_accessed=2 * rows * width * (slot_total + 2 * count + 2),
        ),
        name="layer_rows",
    )(codes, hop_core, *flat, *weights, lists)


def deal_layers(dims, segments, place, near, moved):
    rows, _, width, _, _ = dims
    anyspace = pl.BlockSpec(memory_space=pl.ANY)
    smem = pl.BlockSpec(memory_space=pltpu.SMEM)

    def body(place_ref, *refs):
        ins, refs = refs[: 2 * segments], refs[2 * segments :]
        outs, refs = refs[:segments], refs[segments:]
        hold, sem_in, sem_out = refs
        column = place_ref[0]
        for e in range(2):
            @pl.when(place_ref[1] == e)
            def _():
                for l in range(segments):
                    pltpu.make_async_copy(
                        ins[e * segments + l], hold.at[l], sem_in.at[l]
                    ).start()
        for l in range(segments):
            pltpu.make_async_copy(ins[l], hold.at[l], sem_in.at[l]).wait()
        copies = [
            pltpu.make_async_copy(hold.at[jnp.bitwise_xor(column, h)], outs[h], sem_out.at[h])
            for h in range(segments)
        ]
        for copy in copies:
            copy.start()
        for copy in copies:
            copy.wait()

    return pl.pallas_call(
        body,
        out_shape=[jax.ShapeDtypeStruct((rows, width), jnp.bfloat16)] * segments,
        in_specs=[smem] + [anyspace] * (2 * segments),
        out_specs=[anyspace] * segments,
        scratch_shapes=[
            pltpu.VMEM((segments, rows, width), jnp.bfloat16),
            pltpu.SemaphoreType.DMA((segments,)),
            pltpu.SemaphoreType.DMA((segments,)),
        ],
        name="deal_layers",
    )(place, *near, *moved)


def join_spans(dims, segments, place, pieces):
    rows, _, width, _, _ = dims
    anyspace = pl.BlockSpec(memory_space=pl.ANY)
    smem = pl.BlockSpec(memory_space=pltpu.SMEM)

    def body(place_ref, *refs):
        ins, refs = refs[:segments], refs[segments:]
        out, hold, sem_in, sem_out = refs
        into = [
            pltpu.make_async_copy(ins[h], hold.at[h], sem_in.at[h]) for h in range(segments)
        ]
        away = [
            pltpu.make_async_copy(
                hold.at[h], out.at[jnp.bitwise_xor(place_ref[0], h)], sem_out.at[h]
            )
            for h in range(segments)
        ]
        for copy in into:
            copy.start()
        for first, second in zip(into, away):
            first.wait()
            second.start()
        for copy in away:
            copy.wait()

    return pl.pallas_call(
        body,
        out_shape=jax.ShapeDtypeStruct((segments, rows, width), jnp.bfloat16),
        in_specs=[smem] + [anyspace] * segments,
        out_specs=anyspace,
        scratch_shapes=[
            pltpu.VMEM((segments, rows, width), jnp.bfloat16),
            pltpu.SemaphoreType.DMA((segments,)),
            pltpu.SemaphoreType.DMA((segments,)),
        ],
        name="join_spans",
    )(place, *pieces)


def line_device(
    features, send_rows, send_len, tile_src, tile_count, tile_val, w_self, w_neigh, gain, bias
):
    return line_plan(
        features, send_rows, send_len, tile_src, tile_count, tile_val, w_self, w_neigh, gain, bias
    )


def line_plan(
    features, send_rows, send_len, tile_src, tile_count, tile_val, w_self, w_neigh, gain, bias
):
    segments = lax.axis_size("segment")
    parts = lax.axis_size("dom")
    column = lax.axis_index("segment")
    part = lax.axis_index("dom")
    core = part % 2
    rows, width = features.shape[1:]
    blocks, depth, tile = tile_val.shape[1:4]
    dims = (rows, tile, width, blocks, depth)
    layers = segments
    bf16 = jnp.bfloat16
    mid = [p for p in range(parts) if 0 < p // 2 < parts // 2 - 1]
    rim = [p for p in range(parts) if p not in mid]
    axes = ("segment", "dom")

    def along(array, which, change):
        pairs = [
            (k * parts + p, k * parts + (p ^ change)) for k in range(segments) for p in which
        ]
        return lax.ppermute(array, axes, pairs)

    def across(array, which, change):
        pairs = [
            (k * parts + p, (k ^ change) * parts + p) for k in range(segments) for p in which
        ]
        return lax.ppermute(array, axes, pairs)

    lists = select_span(send_rows, column)[0]
    lens = select_span(send_len, column)[0]
    srcs = select_span(tile_src, column)
    cnts = select_span(tile_count, column)
    live_row = lax.broadcasted_iota(jnp.int32, lists.shape, 1) < lens[:, None]
    lists = jnp.where(live_row, lists + 1, 0).reshape(-1, width)
    live_tile = lax.broadcasted_iota(jnp.int32, srcs.shape, 1) < cnts[:, None]
    codes = jnp.where(live_tile, srcs, 0).reshape(-1)
    codes = jnp.pad(codes, (0, width - codes.shape[0]))[None]
    list_rows = lists.shape[0]
    notes = jnp.concatenate([lists // 16, lists % 16, codes], axis=0)
    notes = jnp.pad(notes, ((0, pad_rows - notes.shape[0]), (0, 0))).astype(bf16)
    feat_own = jnp.concatenate([select_span(features, column), notes], axis=0)
    deep = rows + pad_rows
    val_own = select_span(tile_val, column)
    val_own = jnp.where(live_tile[:, :, None, None], val_own, jnp.zeros_like(val_own))
    val_own = jnp.transpose(val_own, (0, 2, 1, 3)).reshape(blocks * tile, depth * tile)
    both_own = jnp.concatenate([feat_own, val_own], axis=0)

    feat_rim = along(feat_own, rim, 2)
    both_far = along(both_own, mid, 6)
    val_rim = along(val_own, rim, 2)
    feat_far_rim = along(feat_rim, mid, 6)
    val_far_rim = along(val_rim, mid, 6)
    feats = [feat_own, feat_rim, both_far, feat_far_rim]
    feats = feats + [along(a[:deep], mid, 1) for a in feats]
    vals = [(val_own, 0), (val_rim, 0), (both_far, deep), (val_far_rim, 0)]

    tabs = jnp.stack([a[rows : rows + 2 * list_rows + 1] for a in feats]).astype(jnp.int32)
    offs = jnp.array(slot_xor, jnp.int32)
    back = [0] * slot_total
    for n, o in enumerate(slot_xor):
        back[o] = n
    back = jnp.array(back, jnp.int32)
    lists = tabs[:, :list_rows] * 16 + tabs[:, list_rows : 2 * list_rows] - 1
    lists = lists.reshape(slot_total, parts, tile)
    list_cols = jnp.transpose(jnp.take(lists, part ^ offs, axis=1), (1, 2, 0))
    codes = tabs[:, 2 * list_rows, : blocks * depth]
    codes = jnp.where(
        codes < blocks,
        codes,
        blocks + jnp.take(back, jnp.bitwise_xor(jnp.maximum(codes - blocks, 0), part)),
    )
    tables = (codes.reshape(-1), list_cols)

    chosen = jnp.where(core == 0, w_self[0], w_neigh[0])
    filler = jnp.zeros((pad_rows - 2, width), bf16)
    payload = jnp.concatenate([chosen, gain, bias, filler], axis=0)
    mine = jnp.stack([payload] + [across(payload, mid, h) for h in range(1, segments)])
    weights = (mine, along(mine, mid, 1))

    is_rim = jnp.logical_or(part // 2 == 0, part // 2 == parts // 2 - 1)
    every = list(range(parts))
    own, moved = [], []
    x_parts = [(a, 0, (n,)) for n, a in enumerate(feats)]
    last = layers - 1
    for l in range(layers):
        hop_core = jnp.stack([jnp.bitwise_xor(column, l), core]).astype(jnp.int32)
        call = functools.partial(run_layer, dims, tables, weights, hop_core)
        if l < last:
            near, rim_out, full = call(x_parts, vals, 0, ((0,), (1,), (0, 1, 2, 3)))
            swapped = along(full, mid, 1)
            x_parts = [(full, 0, (0, 1, 2, 3)), (swapped, 0, (4, 5, 6, 7))]
        else:
            (rim_out,) = call(x_parts, vals[1:2], 1, ((1,),))
            (near,) = call(x_parts, vals[:1], 0, ((0,),))
        own.append(near)
        moved.append(along(rim_out, mid, 2))

    place = jnp.stack([column, is_rim.astype(jnp.int32)]).astype(jnp.int32)
    dealt = deal_layers(dims, segments, place, own, moved)
    pieces = [dealt[0]] + [across(dealt[h], every, h) for h in range(1, segments)]
    return join_spans(dims, segments, place, pieces)[None]


def solution(mesh):
    in_specs = (
        P(None, "dom", None),
        P(None, "dom", None, None),
        P(None, "dom", None),
        P(None, "dom", None),
        P(None, "dom"),
        P(None, "dom", None, None, None),
        P("segment", None, None),
        P("segment", None, None),
        P("segment", None),
        P("segment", None),
    )
    out_specs = P("segment", None, "dom", None)
    short_line = mesh.shape["dom"] == slot_total and mesh.shape["segment"] == 4
    device = line_device if short_line else general_device
    return jax.shard_map(
        device, mesh=mesh, in_specs=in_specs, out_specs=out_specs, check_vma=False
    )
```

```python
import functools

import jax
import jax.numpy as jnp
from jax import lax
from jax.experimental import pallas as pl
from jax.experimental.pallas import tpu as pltpu
from jax.sharding import PartitionSpec as P


norm_eps = 1e-05
pad_rows = 16


def select_span(array_in, span_id):
    return lax.dynamic_index_in_dim(array_in, span_id, 0, keepdims=False)


def sage_layer(inputs, span_id, graph, w_one, w_two, gain_one, bias_one):
    rows_all, lens_all, src_all, count_all, vals_all = graph
    send_list = select_span(rows_all, span_id)[0]
    send_count = select_span(lens_all, span_id)[0]
    tile_index = select_span(src_all, span_id)
    tile_total = select_span(count_all, span_id)
    tile_vals = select_span(vals_all, span_id)
    peer_count, tile_rows = send_list.shape
    feat_width = inputs.shape[1]
    block_count, tile_depth = tile_index.shape
    picked = jnp.take(inputs, send_list.reshape(-1), axis=0).reshape(
        peer_count, tile_rows, feat_width
    )
    row_live = lax.broadcasted_iota(jnp.int32, (peer_count, tile_rows), 1) < send_count[:, None]
    outgoing = jnp.where(row_live[:, :, None], picked, jnp.zeros_like(picked))
    incoming = lax.all_to_all(outgoing, "dom", split_axis=0, concat_axis=0, tiled=True)
    sources = jnp.concatenate(
        [inputs.reshape(block_count, tile_rows, feat_width), incoming], axis=0
    )
    tile_live = lax.broadcasted_iota(jnp.int32, (block_count, tile_depth), 1) < tile_total[:, None]

    def block_sum(packed):
        block_index, block_vals, block_live = packed
        chosen = jnp.take(sources, block_index, axis=0)
        masked = jnp.where(block_live[:, None, None], block_vals, jnp.zeros_like(block_vals))
        return jnp.einsum("kij,kjd->id", masked, chosen, preferred_element_type=jnp.float32)

    summed = lax.map(block_sum, (tile_index, tile_vals, tile_live))
    gathered = summed.reshape(block_count * tile_rows, feat_width).astype(jnp.bfloat16)
    mixed = jnp.dot(inputs, w_one, preferred_element_type=jnp.float32) + jnp.dot(
        gathered, w_two, preferred_element_type=jnp.float32
    )
    center = mixed - jnp.mean(mixed, axis=1, keepdims=True)
    spread = jnp.mean(center * center, axis=1, keepdims=True)
    scaled = center * lax.rsqrt(spread + norm_eps) * gain_one.astype(jnp.float32) + bias_one.astype(
        jnp.float32
    )
    return jnp.maximum(scaled, 0.0).astype(jnp.bfloat16)


def general_device(
    features, send_rows, send_len, tile_src, tile_count, tile_val, w_self, w_neigh, gain, bias
):
    segments = lax.axis_size("segment")
    segment_id = lax.axis_index("segment")
    span_total = features.shape[0]
    graph = (send_rows, send_len, tile_src, tile_count, tile_val)
    every_self, every_neigh, every_gain, every_bias = (
        lax.all_gather(w_self, "segment", axis=0, tiled=True),
        lax.all_gather(w_neigh, "segment", axis=0, tiled=True),
        lax.all_gather(gain, "segment", axis=0, tiled=True),
        lax.all_gather(bias, "segment", axis=0, tiled=True),
    )
    span_group = span_total // segments
    layers = every_self.shape[0]
    finished = []
    for item in range(span_group):
        span_id = segment_id * span_group + item
        hidden = select_span(features, span_id)
        outputs = []
        for layer_id in range(layers):
            hidden = sage_layer(
                hidden,
                span_id,
                graph,
                every_self[layer_id],
                every_neigh[layer_id],
                every_gain[layer_id],
                every_bias[layer_id],
            )
            outputs.append(hidden)
        finished.append(jnp.stack(outputs))
    dealt_out = jnp.stack(finished, axis=1)
    return lax.all_to_all(dealt_out, "segment", split_axis=0, concat_axis=1, tiled=True)


slot_xor = (0, 2, 6, 4, 1, 3, 7, 5)
slot_total = len(slot_xor)


def layer_body(dims, layer, group, x_spots, t_spots, total_refs, first, out_slots, *refs):
    rows, tile, width, blocks, depth = dims
    count = len(t_spots)
    codes, place = refs[:2]
    refs = refs[2:]
    data, refs = refs[:total_refs], refs[total_refs:]
    mine_w, other_w, list_ref = refs[:3]
    refs = refs[3:]
    o_refs, refs = refs[: len(out_slots)], refs[len(out_slots) :]
    xs, ts, ws, src, agg, ob, sem_x, sem_t, sem_w, sem_o = refs
    hop = jnp.bitwise_xor(place[0], layer)
    core = place[1]

    w_copies = [
        pltpu.make_async_copy(ref.at[hop], ws.at[n], sem_w.at[n])
        for n, ref in enumerate((mine_w, other_w))
    ]
    x_copies = []
    for n, (at, base, slots) in enumerate(x_spots):
        size = len(slots) * rows
        x_copies.append(
            pltpu.make_async_copy(
                data[at].at[pl.ds(base, size), :],
                xs.at[pl.ds(slots[0] * rows, size), :],
                sem_x.at[n],
            )
        )
    t_copies = [
        pltpu.make_async_copy(data[at].at[pl.ds(base, rows), :], ts.at[n], sem_t.at[n])
        for n, (at, base) in enumerate(t_spots)
    ]
    for copy in x_copies + t_copies + w_copies:
        copy.start()
    for copy in x_copies:
        copy.wait()
    lanes = lax.broadcasted_iota(jnp.int32, (tile, rows), 1)

    def start_of(slot):
        return pl.multiple_of(slot * rows, rows)

    def gather(i, u):
        slot = first + i
        src[u, 0:rows, :] = xs[pl.ds(start_of(slot), rows), :]
        lists = list_ref[slot]
        for q in range(slot_total):
            pick = jnp.where(lanes == lists[:, q : q + 1], 1.0, 0.0).astype(jnp.bfloat16)
            block = jnp.dot(
                pick, xs[q * rows : (q + 1) * rows, :], preferred_element_type=jnp.float32
            )
            src[u, rows + q * tile : rows + (q + 1) * tile, :] = block.astype(jnp.bfloat16)

    def sum_tiles(i, u):
        slot = first + i
        for b in range(blocks):
            right = []
            for k in range(depth):
                code = codes[(slot * blocks + b) * depth + k]
                right.append(src[u, pl.ds(pl.multiple_of(code * tile, tile), tile), :])
            total = jnp.dot(
                ts[i, b * tile : (b + 1) * tile, :],
                jnp.concatenate(right, axis=0),
                preferred_element_type=jnp.float32,
            )
            agg[u, b * tile : (b + 1) * tile, :] = total.astype(jnp.bfloat16)

    def project(i, u):
        x = xs[pl.ds(start_of(first + i), rows), :]
        pre = jnp.dot(x, ws[core, :width, :], preferred_element_type=jnp.float32) + jnp.dot(
            agg[u], ws[1 - core, :width, :], preferred_element_type=jnp.float32
        )
        gain_row = ws[0, width : width + 1, :].astype(jnp.float32)
        bias_row = ws[0, width + 1 : width + 2, :].astype(jnp.float32)
        center = pre - jnp.mean(pre, axis=1, keepdims=True)
        spread = jnp.mean(center * center, axis=1, keepdims=True)
        scaled = center * lax.rsqrt(spread + norm_eps) * gain_row + bias_row
        ob[i] = jnp.maximum(scaled, 0.0).astype(jnp.bfloat16)

    def step(j, carry):
        for u in range(group):
            pltpu.make_async_copy(
                data[0].at[pl.ds(0, rows), :], ts.at[j * group + u], sem_t.at[j * group + u]
            ).wait()
        for phase in (gather, sum_tiles):
            for u in range(group):
                phase(j * group + u, u)

        @pl.when(j == 0)
        def _():
            for copy in w_copies:
                copy.wait()

        for u in range(group):
            project(j * group + u, u)
        for n, (ref, slots) in enumerate(zip(o_refs, out_slots)):
            for m, s in enumerate(slots):
                @pl.when(j == (s - first) // group)
                def _():
                    pltpu.make_async_copy(
                        ob.at[s - first], ref.at[pl.ds(m * rows, rows), :], sem_o.at[n, m]
                    ).start()
        return carry

    lax.fori_loop(0, count // group, step, 0)
    for n, (ref, slots) in enumerate(zip(o_refs, out_slots)):
        for m, s in enumerate(slots):
            pltpu.make_async_copy(
                ob.at[s - first], ref.at[pl.ds(m * rows, rows), :], sem_o.at[n, m]
            ).wait()


def run_layer(dims, tables, weights, place, layer, x_parts, t_parts, first, out_slots):
    rows, tile, width, _, depth = dims
    codes, lists = tables
    count = len(t_parts)
    flat = []

    def spot(array):
        for n, have in enumerate(flat):
            if have is array:
                return n
        flat.append(array)
        return len(flat) - 1

    x_spots = tuple((spot(a), base, slots) for a, base, slots in x_parts)
    t_spots = tuple((spot(a), base) for a, base in t_parts)
    anyspace = pl.BlockSpec(memory_space=pl.ANY)
    hbm = pl.BlockSpec(memory_space=pltpu.HBM)
    smem = pl.BlockSpec(memory_space=pltpu.SMEM)
    vmem = pl.BlockSpec(memory_space=pltpu.VMEM)
    bf16 = jnp.bfloat16
    chip_spots = {at for at, _, slots in x_spots if layer > 0}
    data_specs = [anyspace if n in chip_spots else hbm for n in range(len(flat))]
    group = 2 if count % 2 == 0 else 1
    body = functools.partial(
        layer_body, dims, layer, group, x_spots, t_spots, len(flat), first, out_slots
    )
    most = max(len(slots) for slots in out_slots)
    macs = count * rows * width * (2 * width + depth * tile) + count * slot_total * tile * rows * width
    return pl.pallas_call(
        body,
        out_shape=[
            jax.ShapeDtypeStruct((len(slots) * rows, width), bf16) for slots in out_slots
        ],
        in_specs=[smem] * 2 + data_specs + [hbm] * 2 + [vmem],
        out_specs=[anyspace if len(slots) > 1 else hbm for slots in out_slots],
        scratch_shapes=[
            pltpu.VMEM((slot_total * rows, width), bf16),
            pltpu.VMEM((count, rows, depth * tile), bf16),
            pltpu.VMEM((2, width + pad_rows, width), bf16),
            pltpu.VMEM((group, rows + slot_total * tile, width), bf16),
            pltpu.VMEM((group, rows, width), bf16),
            pltpu.VMEM((count, rows, width), bf16),
            pltpu.SemaphoreType.DMA((len(x_parts),)),
            pltpu.SemaphoreType.DMA((count,)),
            pltpu.SemaphoreType.DMA((2,)),
            pltpu.SemaphoreType.DMA((len(out_slots), most)),
        ],
        cost_estimate=pl.CostEstimate(
            flops=2 * macs,
            transcendentals=count * rows,
            bytes_accessed=2 * rows * width * (slot_total + 2 * count + 2),
        ),
        compiler_params=pltpu.CompilerParams(vmem_limit_bytes=((18 if layer else 48) << 20)),
        name="layer_rows",
    )(codes, place, *flat, *weights, lists)


def deal_layers(dims, segments, place, near, moved):
    rows, _, width, _, _ = dims
    size = rows // 2
    hbm = pl.BlockSpec(memory_space=pltpu.HBM)
    smem = pl.BlockSpec(memory_space=pltpu.SMEM)
    spots = list(near) + list(moved)

    def body(place_ref, *refs):
        ins, refs = refs[: 2 * segments], refs[2 * segments :]
        outs, refs = refs[:segments], refs[segments:]
        hold, sem_in, sem_out = refs
        column = place_ref[0]

        def load(e, l):
            n = e * segments + l
            return pltpu.make_async_copy(
                ins[n].at[pl.ds(spots[n][1], size), :], hold.at[l], sem_in.at[l]
            )

        for e in range(2):
            @pl.when(place_ref[2] == e)
            def _():
                for l in range(segments):
                    load(e, l).start()
        for l in range(segments):
            load(0, l).wait()
        copies = [
            pltpu.make_async_copy(hold.at[jnp.bitwise_xor(column, h)], outs[h], sem_out.at[h])
            for h in range(segments)
        ]
        for copy in copies:
            copy.start()
        for copy in copies:
            copy.wait()

    return pl.pallas_call(
        body,
        out_shape=[jax.ShapeDtypeStruct((size, width), jnp.bfloat16)] * segments,
        in_specs=[smem] + [hbm] * (2 * segments),
        out_specs=[hbm] * segments,
        scratch_shapes=[
            pltpu.VMEM((segments, size, width), jnp.bfloat16),
            pltpu.SemaphoreType.DMA((segments,)),
            pltpu.SemaphoreType.DMA((segments,)),
        ],
        compiler_params=pltpu.CompilerParams(vmem_limit_bytes=(24 << 20)),
        name="deal_layers",
    )(place, *[a for a, _ in spots])


def join_spans(dims, segments, place, pieces):
    rows, _, width, _, _ = dims
    hbm = pl.BlockSpec(memory_space=pltpu.HBM)
    smem = pl.BlockSpec(memory_space=pltpu.SMEM)
    size = rows // 2
    order = [(h, m) for m in range(2) for h in range(segments)]

    def body(place_ref, *refs):
        ins, refs = refs[: len(order)], refs[len(order) :]
        out, hold, sem_in, sem_out = refs
        into = []
        away = []
        for n, (h, m) in enumerate(order):
            into.append(pltpu.make_async_copy(ins[n], hold.at[n], sem_in.at[n]))
            target = out.at[jnp.bitwise_xor(place_ref[0], h), pl.ds(m * size, size), :]
            away.append(pltpu.make_async_copy(hold.at[n], target, sem_out.at[n]))
        for copy in into:
            copy.start()
        for first, second in zip(into, away):
            first.wait()
            second.start()
        for copy in away:
            copy.wait()

    return pl.pallas_call(
        body,
        out_shape=jax.ShapeDtypeStruct((segments, rows, width), jnp.bfloat16),
        in_specs=[smem] + [hbm] * len(order),
        out_specs=hbm,
        scratch_shapes=[
            pltpu.VMEM((len(order), size, width), jnp.bfloat16),
            pltpu.SemaphoreType.DMA((len(order),)),
            pltpu.SemaphoreType.DMA((len(order),)),
        ],
        compiler_params=pltpu.CompilerParams(vmem_limit_bytes=(24 << 20)),
        name="join_spans",
    )(place, *[pieces[h][m] for h, m in order])


def line_device(
    features, send_rows, send_len, tile_src, tile_count, tile_val, w_self, w_neigh, gain, bias
):
    return line_plan(
        features, send_rows, send_len, tile_src, tile_count, tile_val, w_self, w_neigh, gain, bias
    )


def line_plan(
    features, send_rows, send_len, tile_src, tile_count, tile_val, w_self, w_neigh, gain, bias
):
    segments = lax.axis_size("segment")
    parts = lax.axis_size("dom")
    column = lax.axis_index("segment")
    part = lax.axis_index("dom")
    core = part % 2
    rows, width = features.shape[1:]
    blocks, depth, tile = tile_val.shape[1:4]
    dims = (rows, tile, width, blocks, depth)
    layers = segments
    bf16 = jnp.bfloat16
    mid = [p for p in range(parts) if 0 < p // 2 < parts // 2 - 1]
    rim = [p for p in range(parts) if p not in mid]
    axes = ("segment", "dom")

    def along(array, which, change):
        pairs = [
            (k * parts + p, k * parts + (p ^ change)) for k in range(segments) for p in which
        ]
        return lax.ppermute(array, axes, pairs)

    def across(array, which, change):
        pairs = [
            (k * parts + p, (k ^ change) * parts + p) for k in range(segments) for p in which
        ]
        return lax.ppermute(array, axes, pairs)

    lists = select_span(send_rows, column)[0]
    lens = select_span(send_len, column)[0]
    srcs = select_span(tile_src, column)
    cnts = select_span(tile_count, column)
    live_row = lax.broadcasted_iota(jnp.int32, lists.shape, 1) < lens[:, None]
    lists = jnp.where(live_row, lists + 1, 0)
    live_tile = lax.broadcasted_iota(jnp.int32, srcs.shape, 1) < cnts[:, None]
    codes = jnp.where(live_tile, srcs, 0)
    codes = jnp.pad(codes, ((0, parts - blocks), (0, tile - depth)))
    spare = jnp.zeros((parts, width - 3 * tile), jnp.int32)
    notes = jnp.concatenate([lists // 16, lists % 16, codes, spare], axis=1).astype(bf16)
    filler = jnp.zeros((pad_rows - parts, width), bf16)
    feat_own = jnp.concatenate([select_span(features, column), notes, filler], axis=0)
    val_own = select_span(tile_val, column)
    val_own = jnp.where(live_tile[:, :, None, None], val_own, jnp.zeros_like(val_own))
    val_own = jnp.transpose(val_own, (0, 2, 1, 3)).reshape(blocks * tile, depth * tile)

    feat_rim = along(feat_own, rim, 2)
    feat_far = along(feat_own, mid, 6)
    val_rim = along(val_own, rim, 2)
    val_far = along(val_own, mid, 6)
    feat_far_rim = along(feat_rim, mid, 6)
    val_far_rim = along(val_rim, mid, 6)
    feats = [feat_own, feat_rim, feat_far, feat_far_rim]
    feats = feats + [along(a, mid, 1) for a in feats]
    vals = [(a, 0) for a in (val_own, val_rim, val_far, val_far_rim)]

    tabs = jnp.stack([a[rows : rows + parts] for a in feats]).astype(jnp.int32)
    offs = jnp.array(slot_xor, jnp.int32)
    back = [0] * slot_total
    for n, o in enumerate(slot_xor):
        back[o] = n
    back = jnp.array(back, jnp.int32)
    lists = tabs[:, :, :tile] * 16 + tabs[:, :, tile : 2 * tile] - 1
    list_cols = jnp.transpose(jnp.take(lists, part ^ offs, axis=1), (1, 2, 0))
    codes = tabs[:, :blocks, 2 * tile : 2 * tile + depth]
    codes = jnp.where(
        codes < blocks,
        codes,
        blocks + jnp.take(back, jnp.bitwise_xor(jnp.maximum(codes - blocks, 0), part)),
    )
    tables = (codes.reshape(-1), list_cols)

    chosen = jnp.where(core == 0, w_self[0], w_neigh[0])
    filler = jnp.zeros((pad_rows - 2, width), bf16)
    payload = jnp.concatenate([chosen, gain, bias, filler], axis=0)
    mine = [payload] + [across(payload, mid, h) for h in range(1, segments)]
    mine = jnp.stack(mine)
    weights = (mine, along(mine, mid, 1))

    is_rim = jnp.logical_or(part // 2 == 0, part // 2 == parts // 2 - 1)
    every = list(range(parts))
    place = jnp.stack([column, core, is_rim.astype(jnp.int32)]).astype(jnp.int32)
    own, moved = [], []
    x_parts = [(a, 0, (n,)) for n, a in enumerate(feats)]
    last = layers - 1
    for l in range(layers):
        call = functools.partial(run_layer, dims, tables, weights, place, l)
        if l < last:
            near, rim_out, full = call(x_parts, vals, 0, ((0,), (1,), (0, 1, 2, 3)))
            swapped = along(full, mid, 1)
            x_parts = [(full, 0, (0, 1, 2, 3)), (swapped, 0, (4, 5, 6, 7))]
        else:
            (rim_out,) = call(x_parts, vals[1:2], 1, ((1,),))
            (near,) = call(x_parts, vals[:1], 0, ((0,),))
        own.append(near)
        if l < last - 1:
            came = along(rim_out, mid, 2)
            moved.append([(came, 0), (came, rows // 2)])
        else:
            parts_out = (rim_out[: rows // 2], rim_out[rows // 2 :])
            moved.append([(along(a, mid, 2), 0) for a in parts_out])

    pieces = [[] for _ in range(segments)]
    for m in range(2):
        base = m * (rows // 2)
        dealt = deal_layers(dims, segments, place, [(a, base) for a in own], [a[m] for a in moved])
        pieces[0].append(dealt[0])
        for h in range(1, segments):
            pieces[h].append(across(dealt[h], every, h))
    return join_spans(dims, segments, place, pieces)[None]


def solution(mesh):
    in_specs = (
        P(None, "dom", None),
        P(None, "dom", None, None),
        P(None, "dom", None),
        P(None, "dom", None),
        P(None, "dom"),
        P(None, "dom", None, None, None),
        P("segment", None, None),
        P("segment", None, None),
        P("segment", None),
        P("segment", None),
    )
    out_specs = P("segment", None, "dom", None)
    short_line = mesh.shape["dom"] == slot_total and mesh.shape["segment"] == 4
    device = line_device if short_line else general_device
    return jax.shard_map(
        device, mesh=mesh, in_specs=in_specs, out_specs=out_specs, check_vma=False
    )
```

```python
import functools

import jax
import jax.numpy as jnp
from jax import lax
from jax.experimental import pallas as pl
from jax.experimental.pallas import tpu as pltpu
from jax.sharding import PartitionSpec as P


norm_eps = 1e-05
pad_rows = 16


def select_span(array_in, span_id):
    return lax.dynamic_index_in_dim(array_in, span_id, 0, keepdims=False)


def sage_layer(inputs, span_id, graph, w_one, w_two, gain_one, bias_one):
    rows_all, lens_all, src_all, count_all, vals_all = graph
    send_list = select_span(rows_all, span_id)[0]
    send_count = select_span(lens_all, span_id)[0]
    tile_index = select_span(src_all, span_id)
    tile_total = select_span(count_all, span_id)
    tile_vals = select_span(vals_all, span_id)
    peer_count, tile_rows = send_list.shape
    feat_width = inputs.shape[1]
    block_count, tile_depth = tile_index.shape
    picked = jnp.take(inputs, send_list.reshape(-1), axis=0).reshape(
        peer_count, tile_rows, feat_width
    )
    row_live = lax.broadcasted_iota(jnp.int32, (peer_count, tile_rows), 1) < send_count[:, None]
    outgoing = jnp.where(row_live[:, :, None], picked, jnp.zeros_like(picked))
    incoming = lax.all_to_all(outgoing, "dom", split_axis=0, concat_axis=0, tiled=True)
    sources = jnp.concatenate(
        [inputs.reshape(block_count, tile_rows, feat_width), incoming], axis=0
    )
    tile_live = lax.broadcasted_iota(jnp.int32, (block_count, tile_depth), 1) < tile_total[:, None]

    def block_sum(packed):
        block_index, block_vals, block_live = packed
        chosen = jnp.take(sources, block_index, axis=0)
        masked = jnp.where(block_live[:, None, None], block_vals, jnp.zeros_like(block_vals))
        return jnp.einsum("kij,kjd->id", masked, chosen, preferred_element_type=jnp.float32)

    summed = lax.map(block_sum, (tile_index, tile_vals, tile_live))
    gathered = summed.reshape(block_count * tile_rows, feat_width).astype(jnp.bfloat16)
    mixed = jnp.dot(inputs, w_one, preferred_element_type=jnp.float32) + jnp.dot(
        gathered, w_two, preferred_element_type=jnp.float32
    )
    center = mixed - jnp.mean(mixed, axis=1, keepdims=True)
    spread = jnp.mean(center * center, axis=1, keepdims=True)
    scaled = center * lax.rsqrt(spread + norm_eps) * gain_one.astype(jnp.float32) + bias_one.astype(
        jnp.float32
    )
    return jnp.maximum(scaled, 0.0).astype(jnp.bfloat16)


def general_device(
    features, send_rows, send_len, tile_src, tile_count, tile_val, w_self, w_neigh, gain, bias
):
    segments = lax.axis_size("segment")
    segment_id = lax.axis_index("segment")
    span_total = features.shape[0]
    graph = (send_rows, send_len, tile_src, tile_count, tile_val)
    every_self, every_neigh, every_gain, every_bias = (
        lax.all_gather(w_self, "segment", axis=0, tiled=True),
        lax.all_gather(w_neigh, "segment", axis=0, tiled=True),
        lax.all_gather(gain, "segment", axis=0, tiled=True),
        lax.all_gather(bias, "segment", axis=0, tiled=True),
    )
    span_group = span_total // segments
    layers = every_self.shape[0]
    finished = []
    for item in range(span_group):
        span_id = segment_id * span_group + item
        hidden = select_span(features, span_id)
        outputs = []
        for layer_id in range(layers):
            hidden = sage_layer(
                hidden,
                span_id,
                graph,
                every_self[layer_id],
                every_neigh[layer_id],
                every_gain[layer_id],
                every_bias[layer_id],
            )
            outputs.append(hidden)
        finished.append(jnp.stack(outputs))
    dealt_out = jnp.stack(finished, axis=1)
    return lax.all_to_all(dealt_out, "segment", split_axis=0, concat_axis=1, tiled=True)


slot_xor = (0, 2, 6, 4, 1, 3, 7, 5)
slot_total = len(slot_xor)
half = slot_total // 2


def layer_body(dims, layer, group, x_spots, t_spots, total_refs, first, out_slots, *refs):
    rows, tile, width, blocks, depth = dims
    count = len(t_spots)
    codes, place = refs[:2]
    refs = refs[2:]
    data, refs = refs[:total_refs], refs[total_refs:]
    w_refs, refs = refs[:2], refs[2:]
    list_ref, refs = refs[0], refs[1:]
    o_refs, refs = refs[: len(out_slots)], refs[len(out_slots) :]
    xs, ts, ws, src, agg, sem_x, sem_t, sem_w = refs
    hop = jnp.bitwise_xor(place[0], layer)
    core = place[1]
    whole = o_refs[-1]

    w_copies = [
        pltpu.make_async_copy(ref.at[hop], ws.at[n], sem_w.at[n]) for n, ref in enumerate(w_refs)
    ]
    x_copies = []
    if layer == 0:
        for n, (at, base, slots) in enumerate(x_spots):
            size = len(slots) * rows
            x_copies.append(
                pltpu.make_async_copy(
                    data[at].at[pl.ds(base, size), :],
                    xs.at[pl.ds(slots[0] * rows, size), :],
                    sem_x.at[n],
                )
            )
    t_copies = [
        pltpu.make_async_copy(data[at].at[pl.ds(base, rows), :], ts.at[n], sem_t.at[n])
        for n, (at, base) in enumerate(t_spots)
    ]
    for copy in x_copies + t_copies + w_copies:
        copy.start()
    for copy in x_copies:
        copy.wait()
    mine_x = xs if layer == 0 else data[x_spots[0][0]]
    other_x = None if layer == 0 else data[x_spots[1][0]]
    lanes = lax.broadcasted_iota(jnp.int32, (tile, rows), 1)

    def start_of(slot):
        return pl.multiple_of(slot * rows, rows)

    def gather(i, u):
        slot = first + i
        src[u, 0:rows, :] = mine_x[pl.ds(start_of(slot), rows), :]
        lists = list_ref[slot]
        for q in range(slot_total):
            pick = jnp.where(lanes == lists[:, q : q + 1], 1.0, 0.0).astype(jnp.bfloat16)
            if layer == 0 or q < half:
                source = mine_x[q * rows : (q + 1) * rows, :]
            else:
                source = other_x[(q - half) * rows : (q - half + 1) * rows, :]
            block = jnp.dot(pick, source, preferred_element_type=jnp.float32)
            src[u, rows + q * tile : rows + (q + 1) * tile, :] = block.astype(jnp.bfloat16)

    def sum_tiles(i, u):
        slot = first + i
        for b in range(blocks):
            right = []
            for k in range(depth):
                code = codes[(slot * blocks + b) * depth + k]
                right.append(src[u, pl.ds(pl.multiple_of(code * tile, tile), tile), :])
            total = jnp.dot(
                ts[i, b * tile : (b + 1) * tile, :],
                jnp.concatenate(right, axis=0),
                preferred_element_type=jnp.float32,
            )
            agg[u, b * tile : (b + 1) * tile, :] = total.astype(jnp.bfloat16)

    def project(i, u):
        x = mine_x[pl.ds(start_of(first + i), rows), :]
        pre = jnp.dot(x, ws[core, :width, :], preferred_element_type=jnp.float32) + jnp.dot(
            agg[u], ws[1 - core, :width, :], preferred_element_type=jnp.float32
        )
        gain_row = ws[0, width : width + 1, :].astype(jnp.float32)
        bias_row = ws[0, width + 1 : width + 2, :].astype(jnp.float32)
        center = pre - jnp.mean(pre, axis=1, keepdims=True)
        spread = jnp.mean(center * center, axis=1, keepdims=True)
        scaled = center * lax.rsqrt(spread + norm_eps) * gain_row + bias_row
        whole[pl.ds(start_of(i), rows), :] = jnp.maximum(scaled, 0.0).astype(jnp.bfloat16)

    def step(j, carry):
        for u in range(group):
            gather(j * group + u, u)
        for u in range(group):
            pltpu.make_async_copy(
                data[t_spots[0][0]].at[pl.ds(0, rows), :],
                ts.at[j * group + u],
                sem_t.at[j * group + u],
            ).wait()
        for u in range(group):
            sum_tiles(j * group + u, u)

        @pl.when(j == 0)
        def _():
            for copy in w_copies:
                copy.wait()

        for u in range(group):
            project(j * group + u, u)
        for ref, (slot,) in zip(o_refs[:-1], out_slots[:-1]):
            @pl.when(j == (slot - first) // group)
            def _():
                ref[...] = whole[(slot - first) * rows : (slot - first + 1) * rows, :]

        return carry

    lax.fori_loop(0, count // group, step, 0)


def run_layer(dims, tables, weights, place, layer, x_parts, t_parts, first, out_slots):
    rows, tile, width, _, depth = dims
    codes, lists = tables
    count = len(t_parts)
    flat = []

    def spot(array):
        for n, have in enumerate(flat):
            if have is array:
                return n
        flat.append(array)
        return len(flat) - 1

    x_spots = tuple((spot(a), base, slots) for a, base, slots in x_parts)
    t_spots = tuple((spot(a), base) for a, base in t_parts)
    hbm = pl.BlockSpec(memory_space=pltpu.HBM)
    smem = pl.BlockSpec(memory_space=pltpu.SMEM)
    vmem = pl.BlockSpec(memory_space=pltpu.VMEM)
    bf16 = jnp.bfloat16
    chip_spots = {at for at, _, slots in x_spots if layer > 0}
    data_specs = [vmem if n in chip_spots else hbm for n in range(len(flat))]
    group = 2 if count % 2 == 0 else 1
    body = functools.partial(
        layer_body, dims, layer, group, x_spots, t_spots, len(flat), first, out_slots
    )
    macs = count * rows * width * (2 * width + depth * tile) + count * slot_total * tile * rows * width
    return pl.pallas_call(
        body,
        out_shape=[
            jax.ShapeDtypeStruct((len(slots) * rows, width), bf16) for slots in out_slots
        ],
        in_specs=[smem] * 2 + data_specs + [hbm] * 2 + [vmem],
        out_specs=[vmem] * len(out_slots),
        scratch_shapes=[
            pltpu.VMEM((slot_total * rows if layer == 0 else rows, width), bf16),
            pltpu.VMEM((count, rows, depth * tile), bf16),
            pltpu.VMEM((2, width + pad_rows, width), bf16),
            pltpu.VMEM((group, rows + slot_total * tile, width), bf16),
            pltpu.VMEM((group, rows, width), bf16),
            pltpu.SemaphoreType.DMA((len(x_parts),)),
            pltpu.SemaphoreType.DMA((count,)),
            pltpu.SemaphoreType.DMA((2,)),
        ],
        cost_estimate=pl.CostEstimate(
            flops=2 * macs,
            transcendentals=count * rows,
            bytes_accessed=2 * rows * width * (slot_total + 2 * count + 2),
        ),
        compiler_params=pltpu.CompilerParams(vmem_limit_bytes=((14 if layer else 48) << 20)),
        name="layer_rows",
    )(codes, place, *flat, *weights, lists)


def deal_layers(dims, segments, place, near, moved):
    rows, _, width, _, _ = dims
    size = rows // 2
    hbm = pl.BlockSpec(memory_space=pltpu.HBM)
    smem = pl.BlockSpec(memory_space=pltpu.SMEM)
    spots = list(near) + list(moved)

    def body(place_ref, *refs):
        ins, refs = refs[: 2 * segments], refs[2 * segments :]
        outs, refs = refs[:segments], refs[segments:]
        hold, sem_in, sem_out = refs
        column = place_ref[0]

        def load(e, l):
            n = e * segments + l
            return pltpu.make_async_copy(
                ins[n].at[pl.ds(spots[n][1], size), :], hold.at[l], sem_in.at[l]
            )

        for e in range(2):
            @pl.when(place_ref[2] == e)
            def _():
                for l in range(segments):
                    load(e, l).start()
        for l in range(segments):
            load(0, l).wait()
        copies = [
            pltpu.make_async_copy(hold.at[jnp.bitwise_xor(column, h)], outs[h], sem_out.at[h])
            for h in range(segments)
        ]
        for copy in copies:
            copy.start()
        for copy in copies:
            copy.wait()

    return pl.pallas_call(
        body,
        out_shape=[jax.ShapeDtypeStruct((size, width), jnp.bfloat16)] * segments,
        in_specs=[smem] + [hbm] * (2 * segments),
        out_specs=[hbm] * segments,
        scratch_shapes=[
            pltpu.VMEM((segments, size, width), jnp.bfloat16),
            pltpu.SemaphoreType.DMA((segments,)),
            pltpu.SemaphoreType.DMA((segments,)),
        ],
        compiler_params=pltpu.CompilerParams(vmem_limit_bytes=(24 << 20)),
        name="deal_layers",
    )(place, *[a for a, _ in spots])


def join_spans(dims, segments, place, pieces):
    rows, _, width, _, _ = dims
    hbm = pl.BlockSpec(memory_space=pltpu.HBM)
    smem = pl.BlockSpec(memory_space=pltpu.SMEM)
    size = rows // 2
    order = [(h, m) for m in range(2) for h in range(segments)]

    def body(place_ref, *refs):
        ins, refs = refs[: len(order)], refs[len(order) :]
        out, hold, sem_in, sem_out = refs
        into = []
        away = []
        for n, (h, m) in enumerate(order):
            into.append(pltpu.make_async_copy(ins[n], hold.at[n], sem_in.at[n]))
            target = out.at[jnp.bitwise_xor(place_ref[0], h), pl.ds(m * size, size), :]
            away.append(pltpu.make_async_copy(hold.at[n], target, sem_out.at[n]))
        for copy in into:
            copy.start()
        for first, second in zip(into, away):
            first.wait()
            second.start()
        for copy in away:
            copy.wait()

    return pl.pallas_call(
        body,
        out_shape=jax.ShapeDtypeStruct((segments, rows, width), jnp.bfloat16),
        in_specs=[smem] + [hbm] * len(order),
        out_specs=hbm,
        scratch_shapes=[
            pltpu.VMEM((len(order), size, width), jnp.bfloat16),
            pltpu.SemaphoreType.DMA((len(order),)),
            pltpu.SemaphoreType.DMA((len(order),)),
        ],
        compiler_params=pltpu.CompilerParams(vmem_limit_bytes=(24 << 20)),
        name="join_spans",
    )(place, *[pieces[h][m] for h, m in order])


def line_device(
    features, send_rows, send_len, tile_src, tile_count, tile_val, w_self, w_neigh, gain, bias
):
    return line_plan(
        features, send_rows, send_len, tile_src, tile_count, tile_val, w_self, w_neigh, gain, bias
    )


def line_plan(
    features, send_rows, send_len, tile_src, tile_count, tile_val, w_self, w_neigh, gain, bias
):
    segments = lax.axis_size("segment")
    parts = lax.axis_size("dom")
    column = lax.axis_index("segment")
    part = lax.axis_index("dom")
    core = part % 2
    rows, width = features.shape[1:]
    blocks, depth, tile = tile_val.shape[1:4]
    dims = (rows, tile, width, blocks, depth)
    layers = segments
    bf16 = jnp.bfloat16
    mid = [p for p in range(parts) if 0 < p // 2 < parts // 2 - 1]
    rim = [p for p in range(parts) if p not in mid]
    axes = ("segment", "dom")

    def along(array, which, change):
        pairs = [
            (k * parts + p, k * parts + (p ^ change)) for k in range(segments) for p in which
        ]
        return lax.ppermute(array, axes, pairs)

    def across(array, which, change):
        pairs = [
            (k * parts + p, (k ^ change) * parts + p) for k in range(segments) for p in which
        ]
        return lax.ppermute(array, axes, pairs)

    lists = select_span(send_rows, column)[0]
    lens = select_span(send_len, column)[0]
    srcs = select_span(tile_src, column)
    cnts = select_span(tile_count, column)
    live_row = lax.broadcasted_iota(jnp.int32, lists.shape, 1) < lens[:, None]
    lists = jnp.where(live_row, lists + 1, 0)
    live_tile = lax.broadcasted_iota(jnp.int32, srcs.shape, 1) < cnts[:, None]
    codes = jnp.where(live_tile, srcs, 0)
    codes = jnp.pad(codes, ((0, parts - blocks), (0, tile - depth)))
    spare = jnp.zeros((parts, width - 3 * tile), jnp.int32)
    notes = jnp.concatenate([lists // 16, lists % 16, codes, spare], axis=1).astype(bf16)
    filler = jnp.zeros((pad_rows - parts, width), bf16)
    feat_own = jnp.concatenate([select_span(features, column), notes, filler], axis=0)
    val_own = select_span(tile_val, column)
    val_own = jnp.where(live_tile[:, :, None, None], val_own, jnp.zeros_like(val_own))
    val_own = jnp.transpose(val_own, (0, 2, 1, 3)).reshape(blocks * tile, depth * tile)

    feat_rim = along(feat_own, rim, 2)
    feat_far = along(feat_own, mid, 6)
    val_rim = along(val_own, rim, 2)
    val_far = along(val_own, mid, 6)
    feat_far_rim = along(feat_rim, mid, 6)
    val_far_rim = along(val_rim, mid, 6)
    feats = [feat_own, feat_rim, feat_far, feat_far_rim]
    feats = feats + [along(a, mid, 1) for a in feats]
    vals = [(a, 0) for a in (val_own, val_rim, val_far, val_far_rim)]

    tabs = jnp.stack([a[rows : rows + parts] for a in feats]).astype(jnp.int32)
    offs = jnp.array(slot_xor, jnp.int32)
    back = [0] * slot_total
    for n, o in enumerate(slot_xor):
        back[o] = n
    back = jnp.array(back, jnp.int32)
    lists = tabs[:, :, :tile] * 16 + tabs[:, :, tile : 2 * tile] - 1
    list_cols = jnp.transpose(jnp.take(lists, part ^ offs, axis=1), (1, 2, 0))
    codes = tabs[:, :blocks, 2 * tile : 2 * tile + depth]
    codes = jnp.where(
        codes < blocks,
        codes,
        blocks + jnp.take(back, jnp.bitwise_xor(jnp.maximum(codes - blocks, 0), part)),
    )
    tables = (codes.reshape(-1), list_cols)

    chosen = jnp.where(core == 0, w_self[0], w_neigh[0])
    filler = jnp.zeros((pad_rows - 2, width), bf16)
    payload = jnp.concatenate([chosen, gain, bias, filler], axis=0)
    mine = [payload] + [across(payload, mid, h) for h in range(1, segments)]
    mine = jnp.stack(mine)
    weights = (mine, along(mine, mid, 1))

    is_rim = jnp.logical_or(part // 2 == 0, part // 2 == parts // 2 - 1)
    every = list(range(parts))
    place = jnp.stack([column, core, is_rim.astype(jnp.int32)]).astype(jnp.int32)
    own, moved = [], []
    x_parts = [(a, 0, (n,)) for n, a in enumerate(feats)]
    last = layers - 1
    for l in range(layers):
        call = functools.partial(run_layer, dims, tables, weights, place, l)
        if l < last:
            near, rim_out, full = call(x_parts, vals, 0, ((0,), (1,), (0, 1, 2, 3)))
            swapped = along(full, mid, 1)
            x_parts = [(full, 0, (0, 1, 2, 3)), (swapped, 0, (4, 5, 6, 7))]
        else:
            (rim_out,) = call(x_parts, vals[1:2], 1, ((1,),))
            (near,) = call(x_parts, vals[:1], 0, ((0,),))
        own.append(near)
        if l < last - 1:
            came = along(rim_out, mid, 2)
            moved.append([(came, 0), (came, rows // 2)])
        else:
            parts_out = (rim_out[: rows // 2], rim_out[rows // 2 :])
            moved.append([(along(a, mid, 2), 0) for a in parts_out])

    pieces = [[] for _ in range(segments)]
    for m in range(2):
        base = m * (rows // 2)
        dealt = deal_layers(dims, segments, place, [(a, base) for a in own], [a[m] for a in moved])
        pieces[0].append(dealt[0])
        for h in range(1, segments):
            pieces[h].append(across(dealt[h], every, h))
    return join_spans(dims, segments, place, pieces)[None]


def solution(mesh):
    in_specs = (
        P(None, "dom", None),
        P(None, "dom", None, None),
        P(None, "dom", None),
        P(None, "dom", None),
        P(None, "dom"),
        P(None, "dom", None, None, None),
        P("segment", None, None),
        P("segment", None, None),
        P("segment", None),
        P("segment", None),
    )
    out_specs = P("segment", None, "dom", None)
    short_line = mesh.shape["dom"] == slot_total and mesh.shape["segment"] == 4
    device = line_device if short_line else general_device
    return jax.shard_map(
        device, mesh=mesh, in_specs=in_specs, out_specs=out_specs, check_vma=False
    )
```

```python
import functools

import jax
import jax.numpy as jnp
from jax import lax
from jax.experimental import pallas as pl
from jax.experimental.pallas import tpu as pltpu
from jax.sharding import PartitionSpec as P


norm_eps = 1e-05
pad_rows = 16


def select_span(array_in, span_id):
    return lax.dynamic_index_in_dim(array_in, span_id, 0, keepdims=False)


def sage_layer(inputs, span_id, graph, w_one, w_two, gain_one, bias_one):
    rows_all, lens_all, src_all, count_all, vals_all = graph
    send_list = select_span(rows_all, span_id)[0]
    send_count = select_span(lens_all, span_id)[0]
    tile_index = select_span(src_all, span_id)
    tile_total = select_span(count_all, span_id)
    tile_vals = select_span(vals_all, span_id)
    peer_count, tile_rows = send_list.shape
    feat_width = inputs.shape[1]
    block_count, tile_depth = tile_index.shape
    picked = jnp.take(inputs, send_list.reshape(-1), axis=0).reshape(
        peer_count, tile_rows, feat_width
    )
    row_live = lax.broadcasted_iota(jnp.int32, (peer_count, tile_rows), 1) < send_count[:, None]
    outgoing = jnp.where(row_live[:, :, None], picked, jnp.zeros_like(picked))
    incoming = lax.all_to_all(outgoing, "dom", split_axis=0, concat_axis=0, tiled=True)
    sources = jnp.concatenate(
        [inputs.reshape(block_count, tile_rows, feat_width), incoming], axis=0
    )
    tile_live = lax.broadcasted_iota(jnp.int32, (block_count, tile_depth), 1) < tile_total[:, None]

    def block_sum(packed):
        block_index, block_vals, block_live = packed
        chosen = jnp.take(sources, block_index, axis=0)
        masked = jnp.where(block_live[:, None, None], block_vals, jnp.zeros_like(block_vals))
        return jnp.einsum("kij,kjd->id", masked, chosen, preferred_element_type=jnp.float32)

    summed = lax.map(block_sum, (tile_index, tile_vals, tile_live))
    gathered = summed.reshape(block_count * tile_rows, feat_width).astype(jnp.bfloat16)
    mixed = jnp.dot(inputs, w_one, preferred_element_type=jnp.float32) + jnp.dot(
        gathered, w_two, preferred_element_type=jnp.float32
    )
    center = mixed - jnp.mean(mixed, axis=1, keepdims=True)
    spread = jnp.mean(center * center, axis=1, keepdims=True)
    scaled = center * lax.rsqrt(spread + norm_eps) * gain_one.astype(jnp.float32) + bias_one.astype(
        jnp.float32
    )
    return jnp.maximum(scaled, 0.0).astype(jnp.bfloat16)


def general_device(
    features, send_rows, send_len, tile_src, tile_count, tile_val, w_self, w_neigh, gain, bias
):
    segments = lax.axis_size("segment")
    segment_id = lax.axis_index("segment")
    span_total = features.shape[0]
    graph = (send_rows, send_len, tile_src, tile_count, tile_val)
    every_self, every_neigh, every_gain, every_bias = (
        lax.all_gather(w_self, "segment", axis=0, tiled=True),
        lax.all_gather(w_neigh, "segment", axis=0, tiled=True),
        lax.all_gather(gain, "segment", axis=0, tiled=True),
        lax.all_gather(bias, "segment", axis=0, tiled=True),
    )
    span_group = span_total // segments
    layers = every_self.shape[0]
    finished = []
    for item in range(span_group):
        span_id = segment_id * span_group + item
        hidden = select_span(features, span_id)
        outputs = []
        for layer_id in range(layers):
            hidden = sage_layer(
                hidden,
                span_id,
                graph,
                every_self[layer_id],
                every_neigh[layer_id],
                every_gain[layer_id],
                every_bias[layer_id],
            )
            outputs.append(hidden)
        finished.append(jnp.stack(outputs))
    dealt_out = jnp.stack(finished, axis=1)
    return lax.all_to_all(dealt_out, "segment", split_axis=0, concat_axis=1, tiled=True)


slot_xor = (0, 2, 6, 4, 1, 3, 7, 5)
slot_total = len(slot_xor)
half = slot_total // 2


def layer_body(dims, layer, group, x_spots, t_spots, total_refs, first, out_slots, *refs):
    rows, tile, width, blocks, depth = dims
    count = len(t_spots)
    codes, place = refs[:2]
    refs = refs[2:]
    data, refs = refs[:total_refs], refs[total_refs:]
    w_refs, refs = refs[:2], refs[2:]
    list_ref, refs = refs[0], refs[1:]
    o_refs, refs = refs[: len(out_slots)], refs[len(out_slots) :]
    xs, ts, ws, src, agg, sem_x, sem_t, sem_w = refs
    hop = jnp.bitwise_xor(place[0], layer)
    core = place[1]
    whole = o_refs[-1]

    w_copies = [
        pltpu.make_async_copy(ref.at[hop], ws.at[n], sem_w.at[n]) for n, ref in enumerate(w_refs)
    ]
    x_copies = []
    if layer == 0:
        for n, (at, base, slots) in enumerate(x_spots):
            size = len(slots) * rows
            x_copies.append(
                pltpu.make_async_copy(
                    data[at].at[pl.ds(base, size), :],
                    xs.at[pl.ds(slots[0] * rows, size), :],
                    sem_x.at[n],
                )
            )
    t_copies = [
        pltpu.make_async_copy(data[at].at[pl.ds(base, rows), :], ts.at[n], sem_t.at[n])
        for n, (at, base) in enumerate(t_spots)
    ]
    for copy in x_copies + t_copies + w_copies:
        copy.start()
    for copy in x_copies:
        copy.wait()
    mine_x = xs if layer == 0 else data[x_spots[0][0]]
    other_x = None if layer == 0 else data[x_spots[1][0]]
    lanes = lax.broadcasted_iota(jnp.int32, (tile, rows), 1)

    def start_of(slot):
        return pl.multiple_of(slot * rows, rows)

    def gather(i, u):
        slot = first + i
        src[u, 0:rows, :] = mine_x[pl.ds(start_of(slot), rows), :]
        lists = list_ref[slot]
        for q in range(slot_total):
            pick = jnp.where(lanes == lists[:, q : q + 1], 1.0, 0.0).astype(jnp.bfloat16)
            if layer == 0 or q < half:
                source = mine_x[q * rows : (q + 1) * rows, :]
            else:
                source = other_x[(q - half) * rows : (q - half + 1) * rows, :]
            block = jnp.dot(pick, source, preferred_element_type=jnp.float32)
            src[u, rows + q * tile : rows + (q + 1) * tile, :] = block.astype(jnp.bfloat16)

    def sum_tiles(i, u):
        slot = first + i
        for b in range(blocks):
            right = []
            for k in range(depth):
                code = codes[(slot * blocks + b) * depth + k]
                right.append(src[u, pl.ds(pl.multiple_of(code * tile, tile), tile), :])
            total = jnp.dot(
                ts[i, b * tile : (b + 1) * tile, :],
                jnp.concatenate(right, axis=0),
                preferred_element_type=jnp.float32,
            )
            agg[u, b * tile : (b + 1) * tile, :] = total.astype(jnp.bfloat16)

    def project(i, u):
        x = mine_x[pl.ds(start_of(first + i), rows), :]
        pre = jnp.dot(x, ws[core, :width, :], preferred_element_type=jnp.float32) + jnp.dot(
            agg[u], ws[1 - core, :width, :], preferred_element_type=jnp.float32
        )
        gain_row = ws[0, width : width + 1, :].astype(jnp.float32)
        bias_row = ws[0, width + 1 : width + 2, :].astype(jnp.float32)
        center = pre - jnp.mean(pre, axis=1, keepdims=True)
        spread = jnp.mean(center * center, axis=1, keepdims=True)
        scaled = center * lax.rsqrt(spread + norm_eps) * gain_row + bias_row
        whole[pl.ds(start_of(i), rows), :] = jnp.maximum(scaled, 0.0).astype(jnp.bfloat16)

    def step(j, carry):
        for u in range(group):
            gather(j * group + u, u)
        for u in range(group):
            pltpu.make_async_copy(
                data[t_spots[0][0]].at[pl.ds(0, rows), :],
                ts.at[j * group + u],
                sem_t.at[j * group + u],
            ).wait()
        for u in range(group):
            sum_tiles(j * group + u, u)

        @pl.when(j == 0)
        def _():
            for copy in w_copies:
                copy.wait()

        for u in range(group):
            project(j * group + u, u)
        for ref, (slot,) in zip(o_refs[:-1], out_slots[:-1]):
            @pl.when(j == (slot - first) // group)
            def _():
                ref[...] = whole[(slot - first) * rows : (slot - first + 1) * rows, :]

        return carry

    lax.fori_loop(0, count // group, step, 0)


def run_layer(dims, tables, weights, place, layer, x_parts, t_parts, first, out_slots):
    rows, tile, width, _, depth = dims
    codes, lists = tables
    count = len(t_parts)
    flat = []

    def spot(array):
        for n, have in enumerate(flat):
            if have is array:
                return n
        flat.append(array)
        return len(flat) - 1

    x_spots = tuple((spot(a), base, slots) for a, base, slots in x_parts)
    t_spots = tuple((spot(a), base) for a, base in t_parts)
    hbm = pl.BlockSpec(memory_space=pltpu.HBM)
    smem = pl.BlockSpec(memory_space=pltpu.SMEM)
    vmem = pl.BlockSpec(memory_space=pltpu.VMEM)
    bf16 = jnp.bfloat16
    chip_spots = {at for at, _, slots in x_spots if layer > 0}
    data_specs = [vmem if n in chip_spots else hbm for n in range(len(flat))]
    group = 2 if count % 2 == 0 else 1
    body = functools.partial(
        layer_body, dims, layer, group, x_spots, t_spots, len(flat), first, out_slots
    )
    macs = count * rows * width * (2 * width + depth * tile) + count * slot_total * tile * rows * width
    return pl.pallas_call(
        body,
        out_shape=[
            jax.ShapeDtypeStruct((len(slots) * rows, width), bf16) for slots in out_slots
        ],
        in_specs=[smem] * 2 + data_specs + [hbm] * 2 + [vmem],
        out_specs=[vmem] * len(out_slots),
        scratch_shapes=[
            pltpu.VMEM((slot_total * rows if layer == 0 else rows, width), bf16),
            pltpu.VMEM((count, rows, depth * tile), bf16),
            pltpu.VMEM((2, width + pad_rows, width), bf16),
            pltpu.VMEM((group, rows + slot_total * tile, width), bf16),
            pltpu.VMEM((group, rows, width), bf16),
            pltpu.SemaphoreType.DMA((len(x_parts),)),
            pltpu.SemaphoreType.DMA((count,)),
            pltpu.SemaphoreType.DMA((2,)),
        ],
        cost_estimate=pl.CostEstimate(
            flops=2 * macs,
            transcendentals=count * rows,
            bytes_accessed=2 * rows * width * (slot_total + 2 * count + 2),
        ),
        compiler_params=pltpu.CompilerParams(vmem_limit_bytes=((14 if layer else 48) << 20)),
        name="layer_rows",
    )(codes, place, *flat, *weights, lists)


def deal_layers(dims, segments, place, near, moved):
    rows, _, width, _, _ = dims
    size = rows // 2
    hbm = pl.BlockSpec(memory_space=pltpu.HBM)
    smem = pl.BlockSpec(memory_space=pltpu.SMEM)
    spots = list(near) + list(moved)

    def body(place_ref, *refs):
        ins, refs = refs[: 2 * segments], refs[2 * segments :]
        outs, refs = refs[:segments], refs[segments:]
        hold, sem_in, sem_out = refs
        column = place_ref[0]

        def load(e, l):
            n = e * segments + l
            return pltpu.make_async_copy(
                ins[n].at[pl.ds(spots[n][1], size), :], hold.at[l], sem_in.at[l]
            )

        for e in range(2):
            @pl.when(place_ref[2] == e)
            def _():
                for l in range(segments):
                    load(e, l).start()
        for l in range(segments):
            load(0, l).wait()
        copies = [
            pltpu.make_async_copy(hold.at[jnp.bitwise_xor(column, h)], outs[h], sem_out.at[h])
            for h in range(segments)
        ]
        for copy in copies:
            copy.start()
        for copy in copies:
            copy.wait()

    return pl.pallas_call(
        body,
        out_shape=[jax.ShapeDtypeStruct((size, width), jnp.bfloat16)] * segments,
        in_specs=[smem] + [hbm] * (2 * segments),
        out_specs=[hbm] * segments,
        scratch_shapes=[
            pltpu.VMEM((segments, size, width), jnp.bfloat16),
            pltpu.SemaphoreType.DMA((segments,)),
            pltpu.SemaphoreType.DMA((segments,)),
        ],
        compiler_params=pltpu.CompilerParams(vmem_limit_bytes=(24 << 20)),
        name="deal_layers",
    )(place, *[a for a, _ in spots])


def join_spans(dims, segments, place, pieces):
    rows, _, width, _, _ = dims
    hbm = pl.BlockSpec(memory_space=pltpu.HBM)
    smem = pl.BlockSpec(memory_space=pltpu.SMEM)
    size = rows // 2
    order = [(h, m) for m in range(2) for h in range(segments)]

    def body(place_ref, *refs):
        ins, refs = refs[: len(order)], refs[len(order) :]
        out, hold, sem_in, sem_out = refs
        into = []
        away = []
        for n, (h, m) in enumerate(order):
            into.append(pltpu.make_async_copy(ins[n], hold.at[n], sem_in.at[n]))
            target = out.at[jnp.bitwise_xor(place_ref[0], h), pl.ds(m * size, size), :]
            away.append(pltpu.make_async_copy(hold.at[n], target, sem_out.at[n]))
        for copy in into:
            copy.start()
        for first, second in zip(into, away):
            first.wait()
            second.start()
        for copy in away:
            copy.wait()

    return pl.pallas_call(
        body,
        out_shape=jax.ShapeDtypeStruct((segments, rows, width), jnp.bfloat16),
        in_specs=[smem] + [hbm] * len(order),
        out_specs=hbm,
        scratch_shapes=[
            pltpu.VMEM((len(order), size, width), jnp.bfloat16),
            pltpu.SemaphoreType.DMA((len(order),)),
            pltpu.SemaphoreType.DMA((len(order),)),
        ],
        compiler_params=pltpu.CompilerParams(vmem_limit_bytes=(24 << 20)),
        name="join_spans",
    )(place, *[pieces[h][m] for h, m in order])


def pack_rows(dims, parts, span, features, send_rows, send_len, tile_src, tile_count):
    rows, tile, width, blocks, depth = dims
    smem = pl.BlockSpec(memory_space=pltpu.SMEM)
    hbm = pl.BlockSpec(memory_space=pltpu.HBM)

    def body(span_ref, lens, srcs, cnts, feats, lists_in, out, hold, lists, sems):
        at = span_ref[0]
        copies = [
            pltpu.make_async_copy(feats.at[at], hold.at[pl.ds(0, rows), :], sems.at[0]),
            pltpu.make_async_copy(lists_in.at[at, 0], lists, sems.at[1]),
        ]
        for copy in copies:
            copy.start()
        row = lax.broadcasted_iota(jnp.int32, (parts, tile), 0)
        lane = lax.broadcasted_iota(jnp.int32, (parts, tile), 1)
        alive = jnp.zeros((parts, tile), jnp.int32)
        for q in range(parts):
            alive = jnp.where(row == q, lens[at, 0, q], alive)
        codes = jnp.zeros((parts, tile), jnp.int32)
        for b in range(blocks):
            for k in range(depth):
                code = jnp.where(k < cnts[at, b], srcs[at, b, k], 0)
                codes = jnp.where((row == b) & (lane == k), code, codes)
        copies[1].wait()
        listed = jnp.where(lane < alive, lists[...] + 1, 0)
        sheet = jnp.concatenate(
            [listed // 16, listed % 16, codes, jnp.zeros((parts, width - 3 * tile), jnp.int32)],
            axis=1,
        )
        sheet = jnp.concatenate([sheet, jnp.zeros((pad_rows - parts, width), jnp.int32)], axis=0)
        hold[rows : rows + pad_rows, :] = sheet.astype(jnp.float32).astype(jnp.bfloat16)
        copies[0].wait()
        away = pltpu.make_async_copy(hold, out, sems.at[2])
        away.start()
        away.wait()

    return pl.pallas_call(
        body,
        out_shape=jax.ShapeDtypeStruct((rows + pad_rows, width), jnp.bfloat16),
        in_specs=[smem] * 4 + [hbm] * 2,
        out_specs=hbm,
        scratch_shapes=[
            pltpu.VMEM((rows + pad_rows, width), jnp.bfloat16),
            pltpu.VMEM((parts, tile), jnp.int32),
            pltpu.SemaphoreType.DMA((3,)),
        ],
        compiler_params=pltpu.CompilerParams(vmem_limit_bytes=(60 << 20)),
        name="pack_rows",
    )(span, send_len, tile_src, tile_count, features, send_rows)


def line_device(
    features, send_rows, send_len, tile_src, tile_count, tile_val, w_self, w_neigh, gain, bias
):
    return line_plan(
        features, send_rows, send_len, tile_src, tile_count, tile_val, w_self, w_neigh, gain, bias
    )


def line_plan(
    features, send_rows, send_len, tile_src, tile_count, tile_val, w_self, w_neigh, gain, bias
):
    segments = lax.axis_size("segment")
    parts = lax.axis_size("dom")
    column = lax.axis_index("segment")
    part = lax.axis_index("dom")
    core = part % 2
    rows, width = features.shape[1:]
    blocks, depth, tile = tile_val.shape[1:4]
    dims = (rows, tile, width, blocks, depth)
    layers = segments
    bf16 = jnp.bfloat16
    mid = [p for p in range(parts) if 0 < p // 2 < parts // 2 - 1]
    rim = [p for p in range(parts) if p not in mid]
    axes = ("segment", "dom")

    def along(array, which, change):
        pairs = [
            (k * parts + p, k * parts + (p ^ change)) for k in range(segments) for p in which
        ]
        return lax.ppermute(array, axes, pairs)

    def across(array, which, change):
        pairs = [
            (k * parts + p, (k ^ change) * parts + p) for k in range(segments) for p in which
        ]
        return lax.ppermute(array, axes, pairs)

    span = column[None].astype(jnp.int32)
    feat_own = pack_rows(dims, parts, span, features, send_rows, send_len, tile_src, tile_count)
    cnts = select_span(tile_count, column)
    live_tile = lax.broadcasted_iota(jnp.int32, (blocks, depth), 1) < cnts[:, None]
    val_own = select_span(tile_val, column)
    val_own = jnp.where(live_tile[:, :, None, None], val_own, jnp.zeros_like(val_own))
    val_own = jnp.transpose(val_own, (0, 2, 1, 3)).reshape(blocks * tile, depth * tile)

    feat_rim = along(feat_own, rim, 2)
    feat_far = along(feat_own, mid, 6)
    val_rim = along(val_own, rim, 2)
    val_far = along(val_own, mid, 6)
    feat_far_rim = along(feat_rim, mid, 6)
    val_far_rim = along(val_rim, mid, 6)
    feats = [feat_own, feat_rim, feat_far, feat_far_rim]
    feats = feats + [along(a, mid, 1) for a in feats]
    vals = [(a, 0) for a in (val_own, val_rim, val_far, val_far_rim)]

    tabs = jnp.stack([a[rows : rows + parts] for a in feats]).astype(jnp.int32)
    offs = jnp.array(slot_xor, jnp.int32)
    back = [0] * slot_total
    for n, o in enumerate(slot_xor):
        back[o] = n
    back = jnp.array(back, jnp.int32)
    lists = tabs[:, :, :tile] * 16 + tabs[:, :, tile : 2 * tile] - 1
    list_cols = jnp.transpose(jnp.take(lists, part ^ offs, axis=1), (1, 2, 0))
    codes = tabs[:, :blocks, 2 * tile : 2 * tile + depth]
    codes = jnp.where(
        codes < blocks,
        codes,
        blocks + jnp.take(back, jnp.bitwise_xor(jnp.maximum(codes - blocks, 0), part)),
    )
    tables = (codes.reshape(-1), list_cols)

    chosen = jnp.where(core == 0, w_self[0], w_neigh[0])
    filler = jnp.zeros((pad_rows - 2, width), bf16)
    payload = jnp.concatenate([chosen, gain, bias, filler], axis=0)
    mine = [payload] + [across(payload, mid, h) for h in range(1, segments)]
    mine = jnp.stack(mine)
    weights = (mine, along(mine, mid, 1))

    is_rim = jnp.logical_or(part // 2 == 0, part // 2 == parts // 2 - 1)
    every = list(range(parts))
    place = jnp.stack([column, core, is_rim.astype(jnp.int32)]).astype(jnp.int32)
    own, moved = [], []
    x_parts = [(a, 0, (n,)) for n, a in enumerate(feats)]
    last = layers - 1
    for l in range(layers):
        call = functools.partial(run_layer, dims, tables, weights, place, l)
        if l < last:
            near, rim_out, full = call(x_parts, vals, 0, ((0,), (1,), (0, 1, 2, 3)))
            swapped = along(full, mid, 1)
            x_parts = [(full, 0, (0, 1, 2, 3)), (swapped, 0, (4, 5, 6, 7))]
        else:
            (rim_out,) = call(x_parts, vals[1:2], 1, ((1,),))
            (near,) = call(x_parts, vals[:1], 0, ((0,),))
        own.append(near)
        if l < last - 1:
            came = along(rim_out, mid, 2)
            moved.append([(came, 0), (came, rows // 2)])
        else:
            parts_out = (rim_out[: rows // 2], rim_out[rows // 2 :])
            moved.append([(along(a, mid, 2), 0) for a in parts_out])

    pieces = [[] for _ in range(segments)]
    for m in range(2):
        base = m * (rows // 2)
        dealt = deal_layers(dims, segments, place, [(a, base) for a in own], [a[m] for a in moved])
        pieces[0].append(dealt[0])
        for h in range(1, segments):
            pieces[h].append(across(dealt[h], every, h))
    return join_spans(dims, segments, place, pieces)[None]


def solution(mesh):
    in_specs = (
        P(None, "dom", None),
        P(None, "dom", None, None),
        P(None, "dom", None),
        P(None, "dom", None),
        P(None, "dom"),
        P(None, "dom", None, None, None),
        P("segment", None, None),
        P("segment", None, None),
        P("segment", None),
        P("segment", None),
    )
    out_specs = P("segment", None, "dom", None)
    short_line = mesh.shape["dom"] == slot_total and mesh.shape["segment"] == 4
    device = line_device if short_line else general_device
    return jax.shard_map(
        device, mesh=mesh, in_specs=in_specs, out_specs=out_specs, check_vma=False
    )
```

```python
import functools

import jax
import jax.numpy as jnp
from jax import lax
from jax.experimental import pallas as pl
from jax.experimental.pallas import tpu as pltpu
from jax.sharding import PartitionSpec as P


norm_eps = 1e-05
pad_rows = 16


def select_span(array_in, span_id):
    return lax.dynamic_index_in_dim(array_in, span_id, 0, keepdims=False)


def sage_layer(inputs, span_id, graph, w_one, w_two, gain_one, bias_one):
    rows_all, lens_all, src_all, count_all, vals_all = graph
    send_list = select_span(rows_all, span_id)[0]
    send_count = select_span(lens_all, span_id)[0]
    tile_index = select_span(src_all, span_id)
    tile_total = select_span(count_all, span_id)
    tile_vals = select_span(vals_all, span_id)
    peer_count, tile_rows = send_list.shape
    feat_width = inputs.shape[1]
    block_count, tile_depth = tile_index.shape
    picked = jnp.take(inputs, send_list.reshape(-1), axis=0).reshape(
        peer_count, tile_rows, feat_width
    )
    row_live = lax.broadcasted_iota(jnp.int32, (peer_count, tile_rows), 1) < send_count[:, None]
    outgoing = jnp.where(row_live[:, :, None], picked, jnp.zeros_like(picked))
    incoming = lax.all_to_all(outgoing, "dom", split_axis=0, concat_axis=0, tiled=True)
    sources = jnp.concatenate(
        [inputs.reshape(block_count, tile_rows, feat_width), incoming], axis=0
    )
    tile_live = lax.broadcasted_iota(jnp.int32, (block_count, tile_depth), 1) < tile_total[:, None]

    def block_sum(packed):
        block_index, block_vals, block_live = packed
        chosen = jnp.take(sources, block_index, axis=0)
        masked = jnp.where(block_live[:, None, None], block_vals, jnp.zeros_like(block_vals))
        return jnp.einsum("kij,kjd->id", masked, chosen, preferred_element_type=jnp.float32)

    summed = lax.map(block_sum, (tile_index, tile_vals, tile_live))
    gathered = summed.reshape(block_count * tile_rows, feat_width).astype(jnp.bfloat16)
    mixed = jnp.dot(inputs, w_one, preferred_element_type=jnp.float32) + jnp.dot(
        gathered, w_two, preferred_element_type=jnp.float32
    )
    center = mixed - jnp.mean(mixed, axis=1, keepdims=True)
    spread = jnp.mean(center * center, axis=1, keepdims=True)
    scaled = center * lax.rsqrt(spread + norm_eps) * gain_one.astype(jnp.float32) + bias_one.astype(
        jnp.float32
    )
    return jnp.maximum(scaled, 0.0).astype(jnp.bfloat16)


def general_device(
    features, send_rows, send_len, tile_src, tile_count, tile_val, w_self, w_neigh, gain, bias
):
    segments = lax.axis_size("segment")
    segment_id = lax.axis_index("segment")
    span_total = features.shape[0]
    graph = (send_rows, send_len, tile_src, tile_count, tile_val)
    every_self, every_neigh, every_gain, every_bias = (
        lax.all_gather(w_self, "segment", axis=0, tiled=True),
        lax.all_gather(w_neigh, "segment", axis=0, tiled=True),
        lax.all_gather(gain, "segment", axis=0, tiled=True),
        lax.all_gather(bias, "segment", axis=0, tiled=True),
    )
    span_group = span_total // segments
    layers = every_self.shape[0]
    finished = []
    for item in range(span_group):
        span_id = segment_id * span_group + item
        hidden = select_span(features, span_id)
        outputs = []
        for layer_id in range(layers):
            hidden = sage_layer(
                hidden,
                span_id,
                graph,
                every_self[layer_id],
                every_neigh[layer_id],
                every_gain[layer_id],
                every_bias[layer_id],
            )
            outputs.append(hidden)
        finished.append(jnp.stack(outputs))
    dealt_out = jnp.stack(finished, axis=1)
    return lax.all_to_all(dealt_out, "segment", split_axis=0, concat_axis=1, tiled=True)


slot_xor = (0, 2, 6, 4, 1, 3, 7, 5)
slot_total = len(slot_xor)
half = slot_total // 2


def layer_body(dims, layer, group, x_spots, t_spots, total_refs, first, out_slots, *refs):
    rows, tile, width, blocks, depth = dims
    count = len(t_spots)
    codes, place = refs[:2]
    refs = refs[2:]
    data, refs = refs[:total_refs], refs[total_refs:]
    w_refs, refs = refs[:2], refs[2:]
    list_ref, refs = refs[0], refs[1:]
    o_refs, refs = refs[: len(out_slots)], refs[len(out_slots) :]
    xs, ts, ws, src, agg, sem_x, sem_t, sem_w = refs
    hop = jnp.bitwise_xor(place[0], layer)
    core = place[1]
    whole = o_refs[-1]
    peel = layer == 0

    w_copies = [
        pltpu.make_async_copy(ref.at[hop], ws.at[n], sem_w.at[n]) for n, ref in enumerate(w_refs)
    ]
    x_copies = []
    if layer == 0:
        for n, (at, base, slots) in enumerate(x_spots):
            size = len(slots) * rows
            x_copies.append(
                pltpu.make_async_copy(
                    data[at].at[pl.ds(base, size), :],
                    xs.at[pl.ds(slots[0] * rows, size), :],
                    sem_x.at[n],
                )
            )
    t_copies = [
        pltpu.make_async_copy(data[at].at[pl.ds(base, rows), :], ts.at[n], sem_t.at[n])
        for n, (at, base) in enumerate(t_spots)
    ]
    for copy in x_copies + t_copies + w_copies:
        copy.start()
    waiting = list(x_copies)
    mine_x = xs if layer == 0 else data[x_spots[0][0]]
    other_x = None if layer == 0 else data[x_spots[1][0]]
    lanes = lax.broadcasted_iota(jnp.int32, (tile, rows), 1)

    def start_of(slot):
        return slot * rows if isinstance(slot, int) else pl.multiple_of(slot * rows, rows)

    def gather(i, u):
        slot = first + i
        if waiting:
            waiting.pop(0).wait()
        src[u, 0:rows, :] = mine_x[pl.ds(start_of(slot), rows), :]
        lists = list_ref[slot]
        for q in range(slot_total):
            pick = jnp.where(lanes == lists[:, q : q + 1], 1.0, 0.0).astype(jnp.bfloat16)
            if waiting and q == len(x_copies) - len(waiting):
                waiting.pop(0).wait()
            if layer == 0 or q < half:
                source = mine_x[q * rows : (q + 1) * rows, :]
            else:
                source = other_x[(q - half) * rows : (q - half + 1) * rows, :]
            block = jnp.dot(pick, source, preferred_element_type=jnp.float32)
            src[u, rows + q * tile : rows + (q + 1) * tile, :] = block.astype(jnp.bfloat16)

    def sum_tiles(i, u):
        slot = first + i
        for b in range(blocks):
            right = []
            for k in range(depth):
                code = codes[(slot * blocks + b) * depth + k]
                right.append(src[u, pl.ds(pl.multiple_of(code * tile, tile), tile), :])
            total = jnp.dot(
                ts[i, b * tile : (b + 1) * tile, :],
                jnp.concatenate(right, axis=0),
                preferred_element_type=jnp.float32,
            )
            agg[u, b * tile : (b + 1) * tile, :] = total.astype(jnp.bfloat16)

    def project(i, u):
        x = mine_x[pl.ds(start_of(first + i), rows), :]
        pre = jnp.dot(x, ws[core, :width, :], preferred_element_type=jnp.float32) + jnp.dot(
            agg[u], ws[1 - core, :width, :], preferred_element_type=jnp.float32
        )
        gain_row = ws[0, width : width + 1, :].astype(jnp.float32)
        bias_row = ws[0, width + 1 : width + 2, :].astype(jnp.float32)
        center = pre - jnp.mean(pre, axis=1, keepdims=True)
        spread = jnp.mean(center * center, axis=1, keepdims=True)
        scaled = center * lax.rsqrt(spread + norm_eps) * gain_row + bias_row
        whole[pl.ds(start_of(i), rows), :] = jnp.maximum(scaled, 0.0).astype(jnp.bfloat16)

    def step(j, carry):
        for u in range(group):
            gather(j * group + u, u)
        for u in range(group):
            pltpu.make_async_copy(
                data[t_spots[0][0]].at[pl.ds(0, rows), :],
                ts.at[j * group + u],
                sem_t.at[j * group + u],
            ).wait()
        for u in range(group):
            sum_tiles(j * group + u, u)

        if isinstance(j, int):
            for copy in w_copies:
                copy.wait()
        elif not peel:
            @pl.when(j == 0)
            def _():
                for copy in w_copies:
                    copy.wait()

        for u in range(group):
            project(j * group + u, u)
        for ref, (slot,) in zip(o_refs[:-1], out_slots[:-1]):
            def keep():
                ref[...] = whole[(slot - first) * rows : (slot - first + 1) * rows, :]

            if not isinstance(j, int):
                if not peel:
                    pl.when(j == (slot - first) // group)(keep)
            elif j == (slot - first) // group:
                keep()
        return carry

    if peel:
        step(0, 0)
        lax.fori_loop(1, count // group, step, 0)
    else:
        lax.fori_loop(0, count // group, step, 0)


def run_layer(dims, tables, weights, place, layer, x_parts, t_parts, first, out_slots):
    rows, tile, width, _, depth = dims
    codes, lists = tables
    count = len(t_parts)
    flat = []

    def spot(array):
        for n, have in enumerate(flat):
            if have is array:
                return n
        flat.append(array)
        return len(flat) - 1

    x_spots = tuple((spot(a), base, slots) for a, base, slots in x_parts)
    t_spots = tuple((spot(a), base) for a, base in t_parts)
    hbm = pl.BlockSpec(memory_space=pltpu.HBM)
    smem = pl.BlockSpec(memory_space=pltpu.SMEM)
    vmem = pl.BlockSpec(memory_space=pltpu.VMEM)
    bf16 = jnp.bfloat16
    chip_spots = {at for at, _, slots in x_spots if layer > 0}
    data_specs = [vmem if n in chip_spots else hbm for n in range(len(flat))]
    group = 2 if count % 2 == 0 else 1
    body = functools.partial(
        layer_body, dims, layer, group, x_spots, t_spots, len(flat), first, out_slots
    )
    macs = count * rows * width * (2 * width + depth * tile) + count * slot_total * tile * rows * width
    return pl.pallas_call(
        body,
        out_shape=[
            jax.ShapeDtypeStruct((len(slots) * rows, width), bf16) for slots in out_slots
        ],
        in_specs=[smem] * 2 + data_specs + [hbm] * 2 + [vmem],
        out_specs=[vmem] * len(out_slots),
        scratch_shapes=[
            pltpu.VMEM((slot_total * rows if layer == 0 else rows, width), bf16),
            pltpu.VMEM((count, rows, depth * tile), bf16),
            pltpu.VMEM((2, width + pad_rows, width), bf16),
            pltpu.VMEM((group, rows + slot_total * tile, width), bf16),
            pltpu.VMEM((group, rows, width), bf16),
            pltpu.SemaphoreType.DMA((len(x_parts),)),
            pltpu.SemaphoreType.DMA((count,)),
            pltpu.SemaphoreType.DMA((2,)),
        ],
        cost_estimate=pl.CostEstimate(
            flops=2 * macs,
            transcendentals=count * rows,
            bytes_accessed=2 * rows * width * (slot_total + 2 * count + 2),
        ),
        compiler_params=pltpu.CompilerParams(vmem_limit_bytes=((14 if layer else 48) << 20)),
        name="layer_rows",
    )(codes, place, *flat, *weights, lists)


def deal_layers(dims, segments, place, near, moved):
    rows, _, width, _, _ = dims
    size = rows // 2
    hbm = pl.BlockSpec(memory_space=pltpu.HBM)
    smem = pl.BlockSpec(memory_space=pltpu.SMEM)
    spots = list(near) + list(moved)

    def body(place_ref, *refs):
        ins, refs = refs[: 2 * segments], refs[2 * segments :]
        outs, refs = refs[:segments], refs[segments:]
        hold, sem_in, sem_out = refs
        column = place_ref[0]

        def load(e, l):
            n = e * segments + l
            return pltpu.make_async_copy(
                ins[n].at[pl.ds(spots[n][1], size), :], hold.at[l], sem_in.at[l]
            )

        for e in range(2):
            @pl.when(place_ref[2] == e)
            def _():
                for l in range(segments):
                    load(e, l).start()
        for l in range(segments):
            load(0, l).wait()
        copies = [
            pltpu.make_async_copy(hold.at[jnp.bitwise_xor(column, h)], outs[h], sem_out.at[h])
            for h in range(segments)
        ]
        for copy in copies:
            copy.start()
        for copy in copies:
            copy.wait()

    return pl.pallas_call(
        body,
        out_shape=[jax.ShapeDtypeStruct((size, width), jnp.bfloat16)] * segments,
        in_specs=[smem] + [hbm] * (2 * segments),
        out_specs=[hbm] * segments,
        scratch_shapes=[
            pltpu.VMEM((segments, size, width), jnp.bfloat16),
            pltpu.SemaphoreType.DMA((segments,)),
            pltpu.SemaphoreType.DMA((segments,)),
        ],
        compiler_params=pltpu.CompilerParams(vmem_limit_bytes=(24 << 20)),
        name="deal_layers",
    )(place, *[a for a, _ in spots])


def join_spans(dims, segments, place, pieces):
    rows, _, width, _, _ = dims
    hbm = pl.BlockSpec(memory_space=pltpu.HBM)
    smem = pl.BlockSpec(memory_space=pltpu.SMEM)
    size = rows // 2
    order = [(h, m) for m in range(2) for h in range(segments)]

    def body(place_ref, *refs):
        ins, refs = refs[: len(order)], refs[len(order) :]
        out, hold, sem_in, sem_out = refs
        into = []
        away = []
        for n, (h, m) in enumerate(order):
            into.append(pltpu.make_async_copy(ins[n], hold.at[n], sem_in.at[n]))
            target = out.at[jnp.bitwise_xor(place_ref[0], h), pl.ds(m * size, size), :]
            away.append(pltpu.make_async_copy(hold.at[n], target, sem_out.at[n]))
        for copy in into:
            copy.start()
        for first, second in zip(into, away):
            first.wait()
            second.start()
        for copy in away:
            copy.wait()

    return pl.pallas_call(
        body,
        out_shape=jax.ShapeDtypeStruct((segments, rows, width), jnp.bfloat16),
        in_specs=[smem] + [hbm] * len(order),
        out_specs=hbm,
        scratch_shapes=[
            pltpu.VMEM((len(order), size, width), jnp.bfloat16),
            pltpu.SemaphoreType.DMA((len(order),)),
            pltpu.SemaphoreType.DMA((len(order),)),
        ],
        compiler_params=pltpu.CompilerParams(vmem_limit_bytes=(24 << 20)),
        name="join_spans",
    )(place, *[pieces[h][m] for h, m in order])


def pack_rows(dims, parts, span, features, send_rows, send_len, tile_src, tile_count):
    rows, tile, width, blocks, depth = dims
    smem = pl.BlockSpec(memory_space=pltpu.SMEM)
    hbm = pl.BlockSpec(memory_space=pltpu.HBM)

    def body(span_ref, lens, srcs, cnts, feats, lists_in, out, hold, lists, sems):
        at = span_ref[0]
        copies = [
            pltpu.make_async_copy(feats.at[at], hold.at[pl.ds(0, rows), :], sems.at[0]),
            pltpu.make_async_copy(lists_in.at[at, 0], lists, sems.at[1]),
        ]
        for copy in copies:
            copy.start()
        row = lax.broadcasted_iota(jnp.int32, (parts, tile), 0)
        lane = lax.broadcasted_iota(jnp.int32, (parts, tile), 1)
        alive = jnp.zeros((parts, tile), jnp.int32)
        for q in range(parts):
            alive = jnp.where(row == q, lens[at, 0, q], alive)
        codes = jnp.zeros((parts, tile), jnp.int32)
        for b in range(blocks):
            for k in range(depth):
                code = jnp.where(k < cnts[at, b], srcs[at, b, k], 0)
                codes = jnp.where((row == b) & (lane == k), code, codes)
        copies[1].wait()
        listed = jnp.where(lane < alive, lists[...] + 1, 0)
        sheet = jnp.concatenate(
            [listed // 16, listed % 16, codes, jnp.zeros((parts, width - 3 * tile), jnp.int32)],
            axis=1,
        )
        sheet = jnp.concatenate([sheet, jnp.zeros((pad_rows - parts, width), jnp.int32)], axis=0)
        hold[rows : rows + pad_rows, :] = sheet.astype(jnp.float32).astype(jnp.bfloat16)
        copies[0].wait()
        away = pltpu.make_async_copy(hold, out, sems.at[2])
        away.start()
        away.wait()

    return pl.pallas_call(
        body,
        out_shape=jax.ShapeDtypeStruct((rows + pad_rows, width), jnp.bfloat16),
        in_specs=[smem] * 4 + [hbm] * 2,
        out_specs=hbm,
        scratch_shapes=[
            pltpu.VMEM((rows + pad_rows, width), jnp.bfloat16),
            pltpu.VMEM((parts, tile), jnp.int32),
            pltpu.SemaphoreType.DMA((3,)),
        ],
        compiler_params=pltpu.CompilerParams(vmem_limit_bytes=(60 << 20)),
        name="pack_rows",
    )(span, send_len, tile_src, tile_count, features, send_rows)


def line_device(
    features, send_rows, send_len, tile_src, tile_count, tile_val, w_self, w_neigh, gain, bias
):
    return line_plan(
        features, send_rows, send_len, tile_src, tile_count, tile_val, w_self, w_neigh, gain, bias
    )


def line_plan(
    features, send_rows, send_len, tile_src, tile_count, tile_val, w_self, w_neigh, gain, bias
):
    segments = lax.axis_size("segment")
    parts = lax.axis_size("dom")
    column = lax.axis_index("segment")
    part = lax.axis_index("dom")
    core = part % 2
    rows, width = features.shape[1:]
    blocks, depth, tile = tile_val.shape[1:4]
    dims = (rows, tile, width, blocks, depth)
    layers = segments
    bf16 = jnp.bfloat16
    mid = [p for p in range(parts) if 0 < p // 2 < parts // 2 - 1]
    rim = [p for p in range(parts) if p not in mid]
    axes = ("segment", "dom")

    def along(array, which, change):
        pairs = [
            (k * parts + p, k * parts + (p ^ change)) for k in range(segments) for p in which
        ]
        return lax.ppermute(array, axes, pairs)

    def across(array, which, change):
        pairs = [
            (k * parts + p, (k ^ change) * parts + p) for k in range(segments) for p in which
        ]
        return lax.ppermute(array, axes, pairs)

    span = column[None].astype(jnp.int32)
    feat_own = pack_rows(dims, parts, span, features, send_rows, send_len, tile_src, tile_count)
    cnts = select_span(tile_count, column)
    live_tile = lax.broadcasted_iota(jnp.int32, (blocks, depth), 1) < cnts[:, None]
    val_own = select_span(tile_val, column)
    val_own = jnp.where(live_tile[:, :, None, None], val_own, jnp.zeros_like(val_own))
    val_own = jnp.transpose(val_own, (0, 2, 1, 3)).reshape(blocks * tile, depth * tile)

    feat_rim = along(feat_own, rim, 2)
    feat_far = along(feat_own, mid, 6)
    val_rim = along(val_own, rim, 2)
    val_far = along(val_own, mid, 6)
    feat_far_rim = along(feat_rim, mid, 6)
    val_far_rim = along(val_rim, mid, 6)
    feats = [feat_own, feat_rim, feat_far, feat_far_rim]
    feats = feats + [along(a, mid, 1) for a in feats]
    vals = [(a, 0) for a in (val_own, val_rim, val_far, val_far_rim)]

    tabs = jnp.stack([a[rows : rows + parts] for a in feats]).astype(jnp.int32)
    offs = jnp.array(slot_xor, jnp.int32)
    back = [0] * slot_total
    for n, o in enumerate(slot_xor):
        back[o] = n
    back = jnp.array(back, jnp.int32)
    lists = tabs[:, :, :tile] * 16 + tabs[:, :, tile : 2 * tile] - 1
    list_cols = jnp.transpose(jnp.take(lists, part ^ offs, axis=1), (1, 2, 0))
    codes = tabs[:, :blocks, 2 * tile : 2 * tile + depth]
    codes = jnp.where(
        codes < blocks,
        codes,
        blocks + jnp.take(back, jnp.bitwise_xor(jnp.maximum(codes - blocks, 0), part)),
    )
    tables = (codes.reshape(-1), list_cols)

    chosen = jnp.where(core == 0, w_self[0], w_neigh[0])
    filler = jnp.zeros((pad_rows - 2, width), bf16)
    payload = jnp.concatenate([chosen, gain, bias, filler], axis=0)
    mine = [payload] + [across(payload, mid, h) for h in range(1, segments)]
    mine = jnp.stack(mine)
    weights = (mine, along(mine, mid, 1))

    is_rim = jnp.logical_or(part // 2 == 0, part // 2 == parts // 2 - 1)
    every = list(range(parts))
    place = jnp.stack([column, core, is_rim.astype(jnp.int32)]).astype(jnp.int32)
    own, moved = [], []
    x_parts = [(a, 0, (n,)) for n, a in enumerate(feats)]
    last = layers - 1
    for l in range(layers):
        call = functools.partial(run_layer, dims, tables, weights, place, l)
        if l < last:
            near, rim_out, full = call(x_parts, vals, 0, ((0,), (1,), (0, 1, 2, 3)))
            swapped = along(full, mid, 1)
            x_parts = [(full, 0, (0, 1, 2, 3)), (swapped, 0, (4, 5, 6, 7))]
        else:
            (rim_out,) = call(x_parts, vals[1:2], 1, ((1,),))
            (near,) = call(x_parts, vals[:1], 0, ((0,),))
        own.append(near)
        if l < last - 1:
            came = along(rim_out, mid, 2)
            moved.append([(came, 0), (came, rows // 2)])
        else:
            parts_out = (rim_out[: rows // 2], rim_out[rows // 2 :])
            moved.append([(along(a, mid, 2), 0) for a in parts_out])

    pieces = [[] for _ in range(segments)]
    for m in range(2):
        base = m * (rows // 2)
        dealt = deal_layers(dims, segments, place, [(a, base) for a in own], [a[m] for a in moved])
        pieces[0].append(dealt[0])
        for h in range(1, segments):
            pieces[h].append(across(dealt[h], every, h))
    return join_spans(dims, segments, place, pieces)[None]


def solution(mesh):
    in_specs = (
        P(None, "dom", None),
        P(None, "dom", None, None),
        P(None, "dom", None),
        P(None, "dom", None),
        P(None, "dom"),
        P(None, "dom", None, None, None),
        P("segment", None, None),
        P("segment", None, None),
        P("segment", None),
        P("segment", None),
    )
    out_specs = P("segment", None, "dom", None)
    short_line = mesh.shape["dom"] == slot_total and mesh.shape["segment"] == 4
    device = line_device if short_line else general_device
    return jax.shard_map(
        device, mesh=mesh, in_specs=in_specs, out_specs=out_specs, check_vma=False
    )
```
